32 devices in a mesh: row: 8 (over y, x, core), col: 4 (over z).
Axes of the slice: x: 2, y: 2, z: 4, core: 2. Of those that a mesh axis runs over, the one named last changes fastest.
Arguments:
- fixed_matrix_encodings: int32 [8192, 53248], P('row', 'col'), may hold values from 0 to 254, as said below
- line_restore_multiplier: float32 [8192], P('row'), may hold values from 0.001 to 0.01
- central_up_matrix: float32 [8192, 16], P('row', 'col'), may hold values from -1.5 to 1.5
- central_down_matrix: float32 [16, 53248], P('row', 'col'), may hold values from -1.5 to 1.5
- running_mean_up: float32 [8192, 16], P('row', 'col'), may hold values from -1.8 to 1.8
- squared_average_up: float32 [8192, 16], P('row', 'col'), may hold values from 0.05 to 0.5
- running_mean_down: float32 [16, 53248], P('row', 'col'), may hold values from -1.8 to 1.8
- squared_average_down: float32 [16, 53248], P('row', 'col'), may hold values from 0.05 to 0.5
- participant_change_up: bfloat16 [32, 8192, 16], P(('row', 'col')), may hold values from -48 to 48
- participant_change_down: bfloat16 [32, 16, 53248], P(('row', 'col')), may hold values from -48 to 48
- client_tallies: int32 [32, 2], P(('row', 'col')), may hold values from 1 to 64
Outputs:
- combined_normalized_entries: bfloat16 [8192, 53248], P('row', 'col')
- fresh_line_multipliers: float32 [8192], P('row')
- lora_b_next: float32 [8192, 16], P('row', 'col')
- lora_a_next: float32 [16, 53248], P('row', 'col')
- moment_b_next: float32 [8192, 16], P('row', 'col')
- second_b_next: float32 [8192, 16], P('row', 'col')
- moment_a_next: float32 [16, 53248], P('row', 'col')
- second_a_next: float32 [16, 53248], P('row', 'col')
The draws below stay inside these ranges and needn't reach their ends.
Inputs may be any that keep to these rules, and one draw needn't show every extreme that they name: `fixed_matrix_encodings`: FP8 e4m3 bit patterns; the not-a-number patterns 127 and 255 never occur.
All inputs are finite; a program needn't handle non-finite values. Where the reference program divides by a largest or mean magnitude, that divisor is 1e-20 or more.
Results may differ from the reference program's by a relative error of at most 0.0053.
Values may be sent and summed in bfloat16 or wider, within the bound.
A program may use at most 192 MiB of HBM per device.

```python
import math
import jax
import jax.numpy as jnp
from jax import lax

EMBED_SPAN = 8192
INNER_NEURONS = 53248
ADAPT_DIMENSION = 16
PARTICIPANTS = 32


def draw_fixed_matrix_encodings(key, part):
    raw = jax.random.randint(key, (EMBED_SPAN, INNER_NEURONS), 0, 254)
    return raw + (raw >= 127).astype(jnp.int32)


def draw_client_tallies(key, part):
    base = jax.random.randint(key, (PARTICIPANTS, 2), 1, 23)
    ramp = 42 * jnp.arange(PARTICIPANTS, dtype=jnp.int32) // max(PARTICIPANTS - 1, 1)
    return base + ramp[:, None]


def spiked(drawn, stream_key, source, target, shards_of, factor):
    def block_of(axis_at):
        return (jnp.arange(drawn.shape[axis_at]) // (drawn.shape[axis_at] // shards_of)).reshape((-1,) + (1,) * (drawn.ndim - 1 - axis_at))

    one_side = jax.random.permutation(stream_key, shards_of)[block_of(target)]
    other_side = (block_of(target) + shards_of // 2) % shards_of
    return jnp.where((block_of(source) == one_side) | (block_of(source) == other_side), factor * drawn, drawn)


def block_scale(key, extent, cuts, smallest, high):
    def one(position, blocks):
        heights = jax.random.uniform(jax.random.fold_in(jax.random.fold_in(key, 6), position), (blocks,), jnp.float32, smallest / len(cuts), high / len(cuts))
        return jnp.repeat(jnp.exp(heights), extent[position] // blocks).reshape((-1,) + (1,) * (len(extent) - position - 1))

    factor_of = one(*cuts[0])
    for cut in cuts[1:]:
        factor_of = factor_of * one(*cut)
    return factor_of


def scatter_about(own_key, shape, spread, limit, shards=(), kind=jnp.bfloat16):
    drawn = spread * jax.random.normal(own_key, shape, jnp.float32)
    if shards:
        drawn = drawn * block_scale(own_key, shape, shards, -0.22, 0.18)
    return jnp.clip(drawn, -limit, limit).astype(kind)


def bell_draw_with(key, extent, width, reach, split, heavy, kind=jnp.bfloat16):
    values = width * jax.random.normal(key, extent, jnp.float32)
    if split:
        values = values * block_scale(key, extent, split, -0.22, 0.18)
    return jnp.clip(spiked(values, jax.random.fold_in(key, 3), *heavy), -reach, reach).astype(kind)


def setup_inputs(seed: int = 0) -> dict:
    splits = jax.random.split(jax.random.key(seed), 12)
    return {
        "fixed_matrix_encodings": draw_fixed_matrix_encodings(jax.random.fold_in(splits[11], 71), 0),
        "line_restore_multiplier": jnp.clip(jnp.exp(math.log(0.01) - 2.30258502 * jax.random.uniform(splits[1], (EMBED_SPAN,), jnp.float32) ** block_scale(splits[1], (EMBED_SPAN,), ((0, 8),), -0.2, 0.2)), 0.001, 0.01),
        "central_up_matrix": scatter_about(splits[2], (EMBED_SPAN, ADAPT_DIMENSION), 0.25, 1.5, ((0, 8), (1, 4)), jnp.float32),
        "central_down_matrix": scatter_about(splits[3], (ADAPT_DIMENSION, INNER_NEURONS), 0.25, 1.5, ((0, 8), (1, 4)), jnp.float32),
        "running_mean_up": scatter_about(splits[4], (EMBED_SPAN, ADAPT_DIMENSION), 0.3, 1.8, ((0, 8), (1, 4)), jnp.float32),
        "squared_average_up": jnp.clip(jnp.exp(math.log(0.5) - 2.3025851 * jax.random.uniform(splits[5], (EMBED_SPAN, ADAPT_DIMENSION), jnp.float32) ** block_scale(splits[5], (EMBED_SPAN, ADAPT_DIMENSION), ((0, 8), (1, 4)), -0.2, 0.2)), 0.05, 0.5),
        "running_mean_down": scatter_about(splits[6], (ADAPT_DIMENSION, INNER_NEURONS), 0.3, 1.8, ((0, 8), (1, 4)), jnp.float32),
        "squared_average_down": jnp.clip(jnp.exp(math.log(0.5) - 2.3025851 * jax.random.uniform(splits[7], (ADAPT_DIMENSION, INNER_NEURONS), jnp.float32) ** block_scale(splits[7], (ADAPT_DIMENSION, INNER_NEURONS), ((0, 8), (1, 4)), -0.2, 0.2)), 0.05, 0.5),
        "participant_change_up": bell_draw_with(splits[8], (PARTICIPANTS, EMBED_SPAN, ADAPT_DIMENSION), 8.0, 48.0, ((0, 32),), (0, 1, 32, 2.75)),
        "participant_change_down": bell_draw_with(splits[9], (PARTICIPANTS, ADAPT_DIMENSION, INNER_NEURONS), 8.0, 48.0, ((0, 32),), (0, 2, 32, 2.75)),
        "client_tallies": draw_client_tallies(jax.random.fold_in(splits[11], 71), 0),
    }


first_decay = 0.9
second_decay = 0.99
server_rate = 0.1
adam_floor = 0.001
adapter_scale = 2.0
count_scale = 64.0
fp8_top = 448.0
peak_eps = 1e-06

def decode(codes):
    sign_bit = codes // 128
    exponent = codes // 8 % 16
    mantissa = codes % 8
    gaussian_sample = (8 + mantissa).astype(jnp.float32) * jnp.exp2((exponent - 10).astype(jnp.float32))
    subnormal = mantissa.astype(jnp.float32) * 2.0 ** (-9)
    magnitude = jnp.where(exponent > 0, gaussian_sample, subnormal)
    return magnitude * (1.0 - 2.0 * sign_bit.astype(jnp.float32))

def adaptive_update(param, moment, second, grad):
    moment_next = first_decay * moment + (1.0 - first_decay) * grad
    second_next = second_decay * second + (1.0 - second_decay) * grad * grad
    param_next = param - server_rate * moment_next / (jnp.sqrt(second_next) + adam_floor)
    return (param_next, moment_next, second_next)

def reference(fixed_matrix_encodings, line_restore_multiplier, central_up_matrix, central_down_matrix, running_mean_up, squared_average_up, running_mean_down, squared_average_down, participant_change_up, participant_change_down, client_tallies):
    weights = client_tallies.astype(jnp.float32) / (count_scale * PARTICIPANTS)
    gradient_b = lax.optimization_barrier(jnp.sum(weights[:, 0, None, None] * participant_change_up.astype(jnp.float32), axis=0))
    gradient_a = lax.optimization_barrier(jnp.sum(weights[:, 1, None, None] * participant_change_down.astype(jnp.float32), axis=0))
    updated_factor_b, updated_moment_b, updated_variance_b = adaptive_update(central_up_matrix, running_mean_up, squared_average_up, gradient_b)
    updated_factor_a, updated_moment_a, updated_variance_a = adaptive_update(central_down_matrix, running_mean_down, squared_average_down, gradient_a)
    thin_up_matrix = updated_factor_b.astype(jnp.bfloat16)
    lowrank_a = updated_factor_a.astype(jnp.bfloat16)
    tile_lines = math.gcd(EMBED_SPAN, 512)
    partition_list = EMBED_SPAN // tile_lines

    def submatrix_piece(pieces):
        codes, scales, left_product = pieces
        decode_weight = decode(codes) * scales[:, None]
        merged_weight = decode_weight + adapter_scale * jnp.dot(left_product, lowrank_a, preferred_element_type=jnp.float32)
        peak = lax.optimization_barrier(jnp.max(jnp.abs(merged_weight), axis=1)) + peak_eps
        return ((merged_weight / peak[:, None]).astype(jnp.bfloat16), peak / fp8_top)
    combined_normalized_entries, fresh_line_multipliers = lax.map(submatrix_piece, (fixed_matrix_encodings.reshape(partition_list, tile_lines, INNER_NEURONS), line_restore_multiplier.reshape(partition_list, tile_lines), thin_up_matrix.reshape(partition_list, tile_lines, ADAPT_DIMENSION)))
    return (combined_normalized_entries.reshape(EMBED_SPAN, INNER_NEURONS), fresh_line_multipliers.reshape(EMBED_SPAN), updated_factor_b, updated_factor_a, updated_moment_b, updated_variance_b, updated_moment_a, updated_variance_a)
```

```python
import functools

import jax
import jax.numpy as jnp
from jax import lax
from jax.experimental import pallas as pl
from jax.experimental.pallas import tpu as pltpu
from jax.sharding import PartitionSpec as P

first_decay = 0.9
second_decay = 0.99
server_rate = 0.1
adam_floor = 0.001
adapter_scale = 2.0
count_scale = 64.0
fp8_top = 448.0
peak_eps = 1e-06
MESH = pl.DeviceIdType.MESH
LANES = 128
decode_lines = 32
merge_lines = 128
code_slots = 3
stage_slots = 2
fetch_lines = 64
fetch_slots = 3
pass_lines = 128
out_lines = 64
out_slots = 3
decode_plan = (3, 1, 1, 1, 2, 1, 1, 1, 1, 2, 2)


def tile_of(width, limit):
    best = LANES
    for tile in range(LANES, limit + 1, LANES):
        if width % tile == 0:
            best = tile
    return best


def adaptive_update(param, moment, second, grad):
    moment_next = first_decay * moment + (1.0 - first_decay) * grad
    second_next = second_decay * second + (1.0 - second_decay) * grad * grad
    param_next = param - server_rate * moment_next / (jnp.sqrt(second_next) + adam_floor)
    return (param_next, moment_next, second_next)


def scaled_decode(codes):
    low = codes & 127
    mantissa = codes & 7
    mantissa = jnp.where(low > 7, mantissa | 8, mantissa)
    magnitude = mantissa << jnp.maximum(low >> 3, 1)
    return jnp.where(codes > 127, -magnitude, magnitude).astype(jnp.float32)


def merge_kernel(
    rows_count, cols_count,
    codes, scale, pb, mb, vb, pa, ma, va, delta_b, delta_a, weight,
    merged, peak_wide, peak_out, nb, nmb, nvb, na, nma, nva,
    dense, code_buf, got_b, got_a, got_w, fac_b, fac_a, all_b, all_a, wide_b, wide_a,
    left, right, stage, scale_wide, top, top_send, got_top,
    code_sem, out_sem, send_sem, recv_sem, gather_send, gather_recv, own_sem,
):
    my_row, my_col = lax.axis_index("row"), lax.axis_index("col")
    count = rows_count * cols_count
    me = my_row * cols_count + my_col
    depth, width = dense.shape
    steps = depth // decode_lines
    tile = tile_of(width, 1024)
    tiles = width // tile
    rank_b, rank_a = pb.shape[0], pa.shape[0]

    def fetch(i):
        slot = lax.rem(i, code_slots)
        return pltpu.make_async_copy(
            codes.at[pl.ds(i * decode_lines, decode_lines)], code_buf.at[slot], code_sem.at[slot]
        )

    for i in range(code_slots):
        fetch(i).start()

    barrier = pltpu.get_barrier_semaphore()

    def greet(k, _):
        to = lax.rem(me + k, count)
        pl.semaphore_signal(
            barrier, inc=1, device_id=(to // cols_count, lax.rem(to, cols_count)), device_id_type=MESH
        )
        return 0

    lax.fori_loop(1, count, greet, 0)
    pl.semaphore_wait(barrier, count - 1)

    def block_a(row, col):
        return delta_a.at[row, :, pl.ds(pl.multiple_of(col * width, LANES), width)]

    def block_b(row, col):
        return delta_b.at[col, :, pl.ds(pl.multiple_of(row * depth, LANES), depth)]

    def exchange(to, source):
        row, col = to // cols_count, lax.rem(to, cols_count)
        parts = (
            (weight, got_w.at[source]),
            (block_b(row, col), got_b.at[source]),
            (block_a(row, col), got_a.at[source]),
        )
        return [
            pltpu.make_async_remote_copy(
                src_ref=src, dst_ref=dst, send_sem=send_sem.at[n, to], recv_sem=recv_sem.at[n, source],
                device_id=(row, col), device_id_type=MESH,
            )
            for n, (src, dst) in enumerate(parts)
        ]

    def send(k, _):
        for copy in exchange(lax.rem(me + k, count), me):
            copy.start()
        return 0

    lax.fori_loop(1, count, send, 0)
    own = [
        pltpu.make_async_copy(weight, got_w.at[me], own_sem.at[0]),
        pltpu.make_async_copy(block_b(my_row, my_col), got_b.at[me], own_sem.at[1]),
        pltpu.make_async_copy(block_a(my_row, my_col), got_a.at[me], own_sem.at[2]),
    ]
    for copy in own:
        copy.start()

    for b in range(depth // LANES):
        line = jnp.broadcast_to(scale[b : b + 1, :] * 2.0 ** (-10), (LANES, LANES))
        scale_wide[b * LANES : (b + 1) * LANES, :] = line.T

    def decode_step(i, _):
        slot = lax.rem(i, code_slots)
        fetch(i).wait()

        def column(j, _):
            at = pl.ds(pl.multiple_of(j * tile, LANES), tile)
            for g in range(decode_lines // 16):
                value = scaled_decode(code_buf[slot, g * 16 : (g + 1) * 16, at])
                dense[pl.ds(pl.multiple_of(i * decode_lines + g * 16, 16), 16), at] = value.astype(
                    jnp.bfloat16
                )
            return 0

        lax.fori_loop(0, tiles, column, 0)

        @pl.when(i + code_slots < steps)
        def _():
            fetch(i + code_slots).start()

        return 0

    lax.fori_loop(0, steps, decode_step, 0)

    for copy in own:
        copy.wait()

    def arrive(k, _):
        source = lax.rem(me + k, count)
        for copy in exchange(source, source):
            copy.wait_recv()
        return 0

    lax.fori_loop(1, count, arrive, 0)

    def summed(got, which, at, shape):
        def add(s, total):
            return total + got_w[s, which : which + 1, 0:1] * got[s, :, at].astype(jnp.float32)

        return lax.fori_loop(0, count, add, jnp.zeros(shape, jnp.float32), unroll=8)

    grad_b = summed(got_b, 0, slice(None), (rank_b, depth))
    p, m, v = adaptive_update(pb[...], mb[...], vb[...], grad_b)
    nb[...] = p
    nmb[...] = m
    nvb[...] = v
    fac_b[...] = p.astype(jnp.bfloat16)

    def gather_b(to, source):
        return pltpu.make_async_remote_copy(
            src_ref=fac_b, dst_ref=all_b.at[source], send_sem=gather_send.at[0, to],
            recv_sem=gather_recv.at[0, source], device_id=(my_row, to), device_id_type=MESH,
        )

    def gather_a(to, source):
        return pltpu.make_async_remote_copy(
            src_ref=fac_a, dst_ref=all_a.at[source], send_sem=gather_send.at[1, to],
            recv_sem=gather_recv.at[1, source], device_id=(to, my_col), device_id_type=MESH,
        )

    for k in range(1, cols_count):
        gather_b(lax.rem(my_col + k, cols_count), my_col).start()
    own_b = pltpu.make_async_copy(fac_b, all_b.at[my_col], own_sem.at[0])
    own_b.start()

    def update_a(j, _):
        at = pl.ds(pl.multiple_of(j * tile, LANES), tile)
        grad = summed(got_a, 1, at, (rank_a, tile))
        p, m, v = adaptive_update(pa[:, at], ma[:, at], va[:, at], grad)
        na[:, at] = p
        nma[:, at] = m
        nva[:, at] = v
        fac_a[:, at] = p.astype(jnp.bfloat16)
        return 0

    lax.fori_loop(0, tiles, update_a, 0)
    for k in range(1, rows_count):
        gather_a(lax.rem(my_row + k, rows_count), my_row).start()
    own_a = pltpu.make_async_copy(fac_a, all_a.at[my_row], own_sem.at[1])
    own_a.start()

    own_b.wait()
    for k in range(1, cols_count):
        source = lax.rem(my_col + k, cols_count)
        gather_b(source, source).wait_recv()
    for c in range(cols_count):
        wide_b[c * rank_b : (c + 1) * rank_b, :] = all_b[c].astype(jnp.float32)
    left[...] = wide_b[...].T.astype(jnp.bfloat16)

    own_a.wait()
    for k in range(1, rows_count):
        source = lax.rem(my_row + k, rows_count)
        gather_a(source, source).wait_recv()

    def assemble(j, _):
        at = pl.ds(pl.multiple_of(j * tile, LANES), tile)
        for r in range(rows_count):
            wide_a[r * rank_a : (r + 1) * rank_a, :] = all_a[r, :, at].astype(jnp.float32)
        right[:, at] = wide_a[...].astype(jnp.bfloat16)
        return 0

    lax.fori_loop(0, tiles, assemble, 0)

    def put(i):
        slot = lax.rem(i, stage_slots)
        lines = pl.ds(pl.multiple_of(i * merge_lines, merge_lines), merge_lines)
        return pltpu.make_async_copy(stage.at[slot], merged.at[lines], out_sem.at[slot])

    merge_steps = depth // merge_lines

    def merge_step(i, _):
        slot = lax.rem(i, stage_slots)
        lines = pl.ds(pl.multiple_of(i * merge_lines, merge_lines), merge_lines)

        @pl.when(i >= stage_slots)
        def _():
            put(i - stage_slots).wait()

        factor = left[lines, :]
        line_scale = scale_wide[lines, :]

        def column(j, highest):
            for t in range(tile // LANES):
                lane = pl.ds(pl.multiple_of(j * tile + t * LANES, LANES), LANES)
                product = jnp.dot(factor, right[:, lane], preferred_element_type=jnp.float32)
                value = dense[lines, lane].astype(jnp.float32) * line_scale
                value = value + adapter_scale * product
                highest = jnp.maximum(highest, jnp.abs(value))
                stage[slot, :, lane] = value.astype(jnp.bfloat16)
            return highest

        top[lines, :] = lax.fori_loop(
            0, tiles, column, jnp.zeros((merge_lines, LANES), jnp.float32)
        )
        put(i).start()
        return 0

    lax.fori_loop(0, merge_steps, merge_step, 0)

    for b in range(depth // LANES):
        square = top[b * LANES : (b + 1) * LANES, :]
        top_send[b : b + 1, :] = jnp.max(square.T, axis=0, keepdims=True)

    def gather_top(to, source):
        return pltpu.make_async_remote_copy(
            src_ref=top_send, dst_ref=got_top.at[source], send_sem=gather_send.at[2, to],
            recv_sem=gather_recv.at[2, source], device_id=(my_row, to), device_id_type=MESH,
        )

    for k in range(1, cols_count):
        gather_top(lax.rem(my_col + k, cols_count), my_col).start()
    peak = top_send[...]
    for k in range(1, cols_count):
        source = lax.rem(my_col + k, cols_count)
        gather_top(source, source).wait_recv()
        peak = jnp.maximum(peak, got_top[source])
    peak = peak + peak_eps
    peak_out[...] = peak / fp8_top
    for b in range(depth // LANES):
        peak_wide[b * LANES : (b + 1) * LANES, :] = jnp.broadcast_to(
            1.0 / peak[b : b + 1, :], (LANES, LANES)
        ).T

    def drain(i, _):
        put(i).wait()
        return 0

    lax.fori_loop(merge_steps - stage_slots, merge_steps, drain, 0)

    def sent(k, _):
        for copy in exchange(lax.rem(me + k, count), me):
            copy.wait_send()
        return 0

    lax.fori_loop(1, count, sent, 0)
    for k in range(1, cols_count):
        to = lax.rem(my_col + k, cols_count)
        gather_b(to, my_col).wait_send()
        gather_top(to, my_col).wait_send()
    for k in range(1, rows_count):
        gather_a(lax.rem(my_row + k, rows_count), my_row).wait_send()


def normalize_kernel(merged, inverse, out):
    for t in range(merged.shape[1] // LANES):
        at = slice(t * LANES, (t + 1) * LANES)
        out[:, at] = (merged[:, at].astype(jnp.float32) * inverse[...]).astype(jnp.bfloat16)


def direct_local(
    fixed_matrix_encodings,
    line_restore_multiplier,
    central_up_matrix,
    central_down_matrix,
    running_mean_up,
    squared_average_up,
    running_mean_down,
    squared_average_down,
    participant_change_up,
    participant_change_down,
    client_tallies,
):
    rows_count = lax.axis_size("row")
    cols_count = lax.axis_size("col")
    count = rows_count * cols_count
    depth, width = fixed_matrix_encodings.shape
    rank_b = central_up_matrix.shape[1]
    rank_a = central_down_matrix.shape[0]
    rank = participant_change_down.shape[1]
    blocks = depth // LANES
    everyone = client_tallies.shape[0] * count
    weights = client_tallies.astype(jnp.float32) / (count_scale * everyone)
    weight = jnp.broadcast_to(weights[0][:, None], (2, LANES))
    delta_b = participant_change_up[0].T.reshape(cols_count, rank_b, depth * rows_count)
    delta_a = participant_change_down[0].reshape(rows_count, rank_a, width * cols_count)
    anywhere = pl.BlockSpec(memory_space=pl.ANY)
    vmem = pl.BlockSpec(memory_space=pltpu.VMEM)
    f32, bf16 = jnp.float32, jnp.bfloat16
    shape = jax.ShapeDtypeStruct
    outs = pl.pallas_call(
        functools.partial(merge_kernel, rows_count, cols_count),
        out_shape=[
            shape((depth, width), bf16),
            shape((depth, LANES), f32),
            shape((blocks, LANES), f32),
        ]
        + [shape((rank_b, depth), f32)] * 3
        + [shape((rank_a, width), f32)] * 3,
        in_specs=[anywhere] + [vmem] * 7 + [anywhere] * 2 + [vmem],
        out_specs=[anywhere] + [vmem] * 8,
        scratch_shapes=[
            pltpu.VMEM((depth, width), bf16),
            pltpu.VMEM((code_slots, decode_lines, width), jnp.int32),
            pltpu.VMEM((count, rank_b, depth), bf16),
            pltpu.VMEM((count, rank_a, width), bf16),
            pltpu.VMEM((count, 2, LANES), f32),
            pltpu.VMEM((rank_b, depth), bf16),
            pltpu.VMEM((rank_a, width), bf16),
            pltpu.VMEM((cols_count, rank_b, depth), bf16),
            pltpu.VMEM((rows_count, rank_a, width), bf16),
            pltpu.VMEM((rank, depth), f32),
            pltpu.VMEM((rank, tile_of(width, 1024)), f32),
            pltpu.VMEM((depth, rank), bf16),
            pltpu.VMEM((rank, width), bf16),
            pltpu.VMEM((stage_slots, merge_lines, width), bf16),
            pltpu.VMEM((depth, LANES), f32),
            pltpu.VMEM((depth, LANES), f32),
            pltpu.VMEM((blocks, LANES), f32),
            pltpu.VMEM((cols_count, blocks, LANES), f32),
            pltpu.SemaphoreType.DMA((code_slots,)),
            pltpu.SemaphoreType.DMA((stage_slots,)),
            pltpu.SemaphoreType.DMA((3, count)),
            pltpu.SemaphoreType.DMA((3, count)),
            pltpu.SemaphoreType.DMA((3, max(rows_count, cols_count))),
            pltpu.SemaphoreType.DMA((3, max(rows_count, cols_count))),
            pltpu.SemaphoreType.DMA((3,)),
        ],
        compiler_params=pltpu.CompilerParams(
            collective_id=0, has_side_effects=True, vmem_limit_bytes=62_000_000
        ),
    )(
        fixed_matrix_encodings,
        line_restore_multiplier.reshape(blocks, LANES),
        central_up_matrix.T,
        running_mean_up.T,
        squared_average_up.T,
        central_down_matrix,
        running_mean_down,
        squared_average_down,
        delta_b,
        delta_a,
        weight,
    )
    merged, inverse, fresh, nb, nmb, nvb, na, nma, nva = outs
    step = 64
    normalized = pl.pallas_call(
        normalize_kernel,
        grid=(depth // step,),
        out_shape=shape((depth, width), bf16),
        in_specs=[
            pl.BlockSpec((step, width), lambda i: (i, 0)),
            pl.BlockSpec((step, LANES), lambda i: (i, 0)),
        ],
        out_specs=pl.BlockSpec((step, width), lambda i: (i, 0)),
    )(merged, inverse)
    return (normalized, fresh.reshape(depth), nb.T, na, nmb.T, nvb.T, nma, nva)


def packed_decode(codes):
    half = jnp.bfloat16
    value = codes.astype(jnp.float32).astype(half)
    negative = value > half(127)
    value = jnp.where(negative, value - half(128), value)
    power = jnp.maximum(jnp.floor(value * half(0.125)) - half(1), half(0))
    value = value - power * half(8)
    return jnp.where(negative, -value, value) * jnp.exp2(power)


def staged_kernel(
    rows_count, cols_count, everyone,
    tallies, codes, scale, pb, mb, vb, pa, ma, va, delta_b, delta_a,
    dense, inverse, fresh, nb, nmb, nvb, na, nma, nva,
    code_buf, weight, got_w, mine_a, core_a, pair_a, chip_a, line_a, got_a, sum_a,
    mine_b, core_b, pair_b, chip_b, line_b, got_b,
    state_a, back_a, wide_a, fac_a, right, fac_b, all_b, wide_b, left, top, top_send, got_top,
    code_sem, own_sem, core_send, core_recv, chip_send, chip_recv, line_send, line_recv,
    state_send, state_recv, back_send, back_recv, row_send, row_recv, col_send, col_recv,
):
    my_row, my_col = lax.axis_index("row"), lax.axis_index("col")
    chips = rows_count // 2
    core, chip = lax.rem(my_row, 2), my_row // 2
    depth, width = dense.shape
    rank = delta_a.shape[0]
    rank_b, rank_a = pb.shape[0], pa.shape[0]
    part = width // rows_count
    half = chips * part
    slot_of = core * chips + chip
    tile = tile_of(width, 1024)
    f32, bf16 = jnp.float32, jnp.bfloat16
    partner = (chip * 2 + 1 - core, my_col)

    def remote(src, dst, send, recv, to):
        return pltpu.make_async_remote_copy(
            src_ref=src, dst_ref=dst, send_sem=send, recv_sem=recv, device_id=to, device_id_type=MESH
        )

    def lanes(start, size):
        return pl.ds(pl.multiple_of(start, LANES), size)

    def fetch(i):
        slot = lax.rem(i, fetch_slots)
        return pltpu.make_async_copy(
            codes.at[pl.ds(i * fetch_lines, fetch_lines)], code_buf.at[slot], code_sem.at[slot]
        )

    steps = depth // fetch_lines
    for i in range(fetch_slots):
        fetch(i).start()

    def own_copies():
        copies = []
        for c in range(cols_count):
            copies.append((delta_a.at[:, lanes(c * width + core * half, half)], mine_a.at[c]))
        for q in range(chips):
            copies.append((delta_b.at[:, lanes((2 * q + core) * depth, depth)], mine_b.at[q]))
        for n, state in enumerate((pa, ma, va)):
            copies.append((state.at[:, lanes(slot_of * part, part)], state_a.at[n, my_row]))
        return [pltpu.make_async_copy(s, d, own_sem.at[n]) for n, (s, d) in enumerate(copies)]

    own = own_copies()
    for copy in own:
        copy.start()

    for n in range(2):
        portion = tallies[0, n].astype(f32) / (count_scale * everyone)
        weight[n * 8 : (n + 1) * 8, :] = jnp.full((8, LANES), portion, f32)

    barrier = pltpu.get_barrier_semaphore()
    for k in range(1, rows_count):
        pl.semaphore_signal(
            barrier, inc=1, device_id=(lax.rem(my_row + k, rows_count), my_col), device_id_type=MESH
        )
    for k in range(1, cols_count):
        pl.semaphore_signal(
            barrier, inc=1, device_id=(my_row, lax.rem(my_col + k, cols_count)), device_id_type=MESH
        )
    pl.semaphore_wait(barrier, rows_count + cols_count - 2)

    def core_copy_a(c):
        return remote(
            delta_a.at[:, lanes(c * width + (1 - core) * half, half)], core_a.at[c],
            core_send.at[c], core_recv.at[c], partner,
        )

    def core_copy_b(q):
        return remote(
            delta_b.at[:, lanes((2 * q + 1 - core) * depth, depth)], core_b.at[q],
            core_send.at[cols_count + q], core_recv.at[cols_count + q], partner,
        )

    last = cols_count + chips
    core_copy_w = remote(weight, got_w, core_send.at[last], core_recv.at[last], partner)

    def state_copy(n, to, source):
        piece = lax.rem(to, 2) * chips + to // 2
        return remote(
            (pa, ma, va)[n].at[:, lanes(piece * part, part)], state_a.at[n, source],
            state_send.at[n, to], state_recv.at[n, source], (to, my_col),
        )

    core_copy_w.start()
    for k in range(1, cols_count + 1):
        core_copy_a(lax.rem(my_col + k, cols_count)).start()
    for q in range(chips):
        core_copy_b(q).start()
    for k in range(1, rows_count):
        for n in range(3):
            state_copy(n, lax.rem(my_row + k, rows_count), my_row).start()

    def decode_step(i, _):
        slot = lax.rem(i, fetch_slots)
        fetch(i).wait()

        def column(j, _):
            at = lanes(j * tile, tile)
            for g in range(fetch_lines // 16):
                dense[pl.ds(pl.multiple_of(i * fetch_lines + g * 16, 16), 16), at] = packed_decode(
                    code_buf[slot, g * 16 : (g + 1) * 16, at]
                )
            return 0

        lax.fori_loop(0, width // tile, column, 0)

        @pl.when(i + fetch_slots < steps)
        def _():
            fetch(i + fetch_slots).start()

        return 0

    done = [0]
    plan = list(decode_plan)

    def decode_some():
        until = min(steps, done[0] + plan.pop(0)) if plan else steps
        if until > done[0]:
            lax.fori_loop(done[0], until, decode_step, 0)
        done[0] = until

    decode_some()

    for copy in own:
        copy.wait()
    core_copy_w.wait_recv()

    def blend(mine, theirs, which):
        ours = weight[which * 8 : which * 8 + 1, 0:1] * mine.astype(f32)
        return (ours + got_w[which * 8 : which * 8 + 1, 0:1] * theirs.astype(f32)).astype(bf16)

    def chip_copy_a(q, c, source):
        return remote(
            pair_a.at[q, c], chip_a.at[source, c], chip_send.at[q, c], chip_recv.at[source, c],
            (q * 2 + core, my_col),
        )

    def chip_copy_b(q, source):
        return remote(
            pair_b.at[q], chip_b.at[source], chip_send.at[q, cols_count],
            chip_recv.at[source, cols_count], (q * 2 + core, my_col),
        )

    for q in range(chips):
        core_copy_b(q).wait_recv()
    for q in range(chips):
        pair_b[q] = blend(mine_b[q], core_b[q], 0)
    for k in range(1, chips):
        chip_copy_b(lax.rem(chip + k, chips), chip).start()
    for k in range(1, cols_count + 1):
        c = lax.rem(my_col + k, cols_count)
        core_copy_a(c).wait_recv()
        for q in range(chips):
            at = slice(q * part, (q + 1) * part)
            pair_a[q, c] = blend(mine_a[c, :, at], core_a[c, :, at], 1)
        for j in range(1, chips):
            chip_copy_a(lax.rem(chip + j, chips), c, chip).start()
        decode_some()

    def line_copy_a(c, source):
        return remote(
            line_a.at[c], got_a.at[source], line_send.at[0, c], line_recv.at[0, source], (my_row, c)
        )

    def line_copy_b(c, source):
        return remote(
            line_b.at[c], got_b.at[source], line_send.at[1, c], line_recv.at[1, source], (my_row, c)
        )

    total = pair_b[chip].astype(f32)
    for k in range(1, chips):
        source = lax.rem(chip + k, chips)
        chip_copy_b(source, source).wait_recv()
        total = total + chip_b[source].astype(f32)
    for c in range(cols_count):
        line_b[c] = total[c * rank_b : (c + 1) * rank_b, :]
    for k in range(1, cols_count):
        line_copy_b(lax.rem(my_col + k, cols_count), my_col).start()

    for k in range(1, cols_count + 1):
        c = lax.rem(my_col + k, cols_count)
        total = pair_a[chip, c].astype(f32)
        for j in range(1, chips):
            source = lax.rem(chip + j, chips)
            chip_copy_a(source, c, source).wait_recv()
            total = total + chip_a[source, c].astype(f32)
        if k < cols_count:
            line_a[c] = total.astype(bf16)
            line_copy_a(c, my_col).start()
            decode_some()
        else:
            sum_a[...] = total

    decode_some()

    grad = line_b[my_col]
    for k in range(1, cols_count):
        source = lax.rem(my_col + k, cols_count)
        line_copy_b(source, source).wait_recv()
        grad = grad + got_b[source]
    p, m, v = adaptive_update(pb[...], mb[...], vb[...], grad)
    nb[...] = p
    nmb[...] = m
    nvb[...] = v
    fac_b[...] = p.astype(bf16)

    def gather_b(to, source):
        return remote(
            fac_b, all_b.at[source], col_send.at[0, to], col_recv.at[0, source], (my_row, to)
        )

    for k in range(1, cols_count):
        gather_b(lax.rem(my_col + k, cols_count), my_col).start()

    for k in range(1, rows_count):
        for n in range(3):
            source = lax.rem(my_row + k, rows_count)
            state_copy(n, source, source).wait_recv()
    for k in range(1, cols_count):
        source = lax.rem(my_col + k, cols_count)
        line_copy_a(source, source).wait_recv()

    grad = sum_a[...]
    for k in range(1, cols_count):
        grad = grad + got_a[lax.rem(my_col + k, cols_count)].astype(f32)
    for r in range(rows_count):
        at = slice(r * rank_a, (r + 1) * rank_a)
        p, m, v = adaptive_update(state_a[0, r], state_a[1, r], state_a[2, r], grad[at, :])
        back_a[0, r] = p
        back_a[1, r] = m
        back_a[2, r] = v
        wide_a[at, :] = p
    fac_a[...] = wide_a[...].astype(bf16)

    def right_at(row):
        piece = lax.rem(row, 2) * chips + row // 2
        return right.at[0:rank, lanes(piece * part, part)]

    def gather_a(to, source):
        return remote(
            fac_a, right_at(source), row_send.at[to], row_recv.at[source], (to, my_col)
        )

    def back_copy(n, to, source):
        piece = lax.rem(source, 2) * chips + source // 2
        return remote(
            back_a.at[n, to], (na, nma, nva)[n].at[:, lanes(piece * part, part)],
            back_send.at[n, to], back_recv.at[n, source], (to, my_col),
        )

    for k in range(1, rows_count):
        gather_a(lax.rem(my_row + k, rows_count), my_row).start()
    own_right = pltpu.make_async_copy(fac_a, right_at(my_row), own_sem.at[0])
    own_right.start()
    own_factor = pltpu.make_async_copy(fac_b, all_b.at[my_col], own_sem.at[1])
    own_factor.start()
    own_back = [
        pltpu.make_async_copy(
            back_a.at[n, my_row], ref.at[:, lanes(slot_of * part, part)], own_sem.at[2 + n]
        )
        for n, ref in enumerate((na, nma, nva))
    ]
    for copy in own_back:
        copy.start()
    for k in range(1, rows_count):
        for n in range(3):
            back_copy(n, lax.rem(my_row + k, rows_count), my_row).start()

    plan[:] = []
    decode_some()

    own_factor.wait()
    for k in range(1, cols_count):
        source = lax.rem(my_col + k, cols_count)
        gather_b(source, source).wait_recv()
    for c in range(cols_count):
        wide_b[c * rank_b : (c + 1) * rank_b, :] = all_b[c].astype(f32)
    for b in range(depth // LANES):
        at = slice(b * LANES, (b + 1) * LANES)
        folded = wide_b[0:rank, at] * (adapter_scale * 2.0**9 / scale[b : b + 1, :])
        high = folded.astype(bf16).astype(f32)
        wide_b[0:rank, at] = high
        wide_b[rank : 2 * rank, at] = folded - high
    left[...] = wide_b[...].T.astype(bf16)

    own_right.wait()
    for k in range(1, rows_count):
        source = lax.rem(my_row + k, rows_count)
        gather_a(source, source).wait_recv()

    def repeat(j, _):
        at = lanes(j * tile, tile)
        right[rank : 2 * rank, at] = right[0:rank, at]
        return 0

    lax.fori_loop(0, width // tile, repeat, 0)

    def merge_step(i, _):
        lines = pl.ds(pl.multiple_of(i * pass_lines, pass_lines), pass_lines)
        factor = left[lines, :]

        def column(j, highest):
            for t in range(tile // LANES):
                lane = lanes(j * tile + t * LANES, LANES)
                value = jnp.dot(factor, right[:, lane], preferred_element_type=f32)
                value = value + dense[lines, lane].astype(f32)
                highest = jnp.maximum(highest, jnp.abs(value))
                dense[lines, lane] = value.astype(bf16)
            return highest

        top[lines, :] = lax.fori_loop(
            0, width // tile, column, jnp.zeros((pass_lines, LANES), f32)
        )
        return 0

    lax.fori_loop(0, depth // pass_lines, merge_step, 0)

    for b in range(depth // LANES):
        square = top[b * LANES : (b + 1) * LANES, :]
        top_send[b : b + 1, :] = jnp.max(square.T, axis=0, keepdims=True)

    def gather_top(to, source):
        return remote(
            top_send, got_top.at[source], col_send.at[1, to], col_recv.at[1, source], (my_row, to)
        )

    for k in range(1, cols_count):
        gather_top(lax.rem(my_col + k, cols_count), my_col).start()
    peak = top_send[...]
    for k in range(1, cols_count):
        source = lax.rem(my_col + k, cols_count)
        gather_top(source, source).wait_recv()
        peak = jnp.maximum(peak, got_top[source])
    unit = scale[...] * 2.0 ** (-9)
    peak = peak * unit + peak_eps
    fresh[...] = peak / fp8_top
    ratio = unit / peak
    for b in range(depth // LANES):
        inverse[b * LANES : (b + 1) * LANES, :] = jnp.broadcast_to(
            ratio[b : b + 1, :], (LANES, LANES)
        ).T

    for copy in own_back:
        copy.wait()
    core_copy_w.wait_send()
    for c in range(cols_count):
        core_copy_a(c).wait_send()
    for q in range(chips):
        core_copy_b(q).wait_send()
    for k in range(1, chips):
        q = lax.rem(chip + k, chips)
        chip_copy_b(q, chip).wait_send()
        for c in range(cols_count):
            chip_copy_a(q, c, chip).wait_send()
    for k in range(1, cols_count):
        to = lax.rem(my_col + k, cols_count)
        line_copy_a(to, my_col).wait_send()
        line_copy_b(to, my_col).wait_send()
        gather_b(to, my_col).wait_send()
        gather_top(to, my_col).wait_send()
    for k in range(1, rows_count):
        to = lax.rem(my_row + k, rows_count)
        gather_a(to, my_row).wait_send()
        for n in range(3):
            state_copy(n, to, my_row).wait_send()
            back_copy(n, to, to).wait_recv()
            back_copy(n, to, my_row).wait_send()


def finish_kernel(small, merged, inverse, *refs):
    ins, out, outs = refs[:small], refs[small], refs[small + 1 : 2 * small + 1]
    stage, out_sem, small_sem = refs[2 * small + 1 :]
    depth, width = merged.shape
    tile = tile_of(width, 1024)
    copies = [
        pltpu.make_async_copy(src, dst, small_sem.at[n]) for n, (src, dst) in enumerate(zip(ins, outs))
    ]
    for copy in copies:
        copy.start()

    def put(i):
        slot = lax.rem(i, out_slots)
        return pltpu.make_async_copy(
            stage.at[slot], out.at[pl.ds(pl.multiple_of(i * out_lines, out_lines), out_lines)], out_sem.at[slot]
        )

    steps = depth // out_lines

    def step(i, _):
        slot = lax.rem(i, out_slots)

        @pl.when(i >= out_slots)
        def _():
            put(i - out_slots).wait()

        lines = pl.ds(pl.multiple_of(i * out_lines, out_lines), out_lines)
        factor = inverse[lines, :]

        def column(j, _):
            for t in range(tile // LANES):
                at = pl.ds(pl.multiple_of(j * tile + t * LANES, LANES), LANES)
                stage[slot, :, at] = (merged[lines, at].astype(jnp.float32) * factor).astype(jnp.bfloat16)
            return 0

        lax.fori_loop(0, width // tile, column, 0)
        put(i).start()
        return 0

    lax.fori_loop(0, steps, step, 0)

    def drain(i, _):
        put(i).wait()
        return 0

    lax.fori_loop(steps - out_slots, steps, drain, 0)
    for copy in copies:
        copy.wait()


def staged_local(
    fixed_matrix_encodings,
    line_restore_multiplier,
    central_up_matrix,
    central_down_matrix,
    running_mean_up,
    squared_average_up,
    running_mean_down,
    squared_average_down,
    participant_change_up,
    participant_change_down,
    client_tallies,
):
    rows_count = lax.axis_size("row")
    cols_count = lax.axis_size("col")
    count = rows_count * cols_count
    depth, width = fixed_matrix_encodings.shape
    rank_b = central_up_matrix.shape[1]
    rank_a = central_down_matrix.shape[0]
    rank = participant_change_down.shape[1]
    blocks = depth // LANES
    chips = rows_count // 2
    part = width // rows_count
    half = chips * part
    everyone = client_tallies.shape[0] * count
    anywhere = pl.BlockSpec(memory_space=pl.ANY)
    vmem = pl.BlockSpec(memory_space=pltpu.VMEM)
    f32, bf16 = jnp.float32, jnp.bfloat16
    here = pltpu.VMEM
    dma = pltpu.SemaphoreType.DMA
    small_shapes = [(blocks, LANES)] + [(rank_b, depth)] * 3 + [(rank_a, width)] * 3
    outs = pl.pallas_call(
        functools.partial(staged_kernel, rows_count, cols_count, everyone),
        out_shape=[here((depth, width), bf16), here((depth, LANES), f32)]
        + [here(shape, f32) for shape in small_shapes],
        in_specs=[pl.BlockSpec(memory_space=pltpu.SMEM), anywhere] + [vmem] * 7 + [anywhere] * 2,
        out_specs=[vmem] * 9,
        scratch_shapes=[
            here((fetch_slots, fetch_lines, width), jnp.int32),
            here((16, LANES), f32),
            here((16, LANES), f32),
            here((cols_count, rank, half), bf16),
            here((cols_count, rank, half), bf16),
            here((chips, cols_count, rank, part), bf16),
            here((chips, cols_count, rank, part), bf16),
            here((cols_count, rank, part), bf16),
            here((cols_count, rank, part), bf16),
            here((rank, part), f32),
            here((chips, rank, depth), bf16),
            here((chips, rank, depth), bf16),
            here((chips, rank, depth), bf16),
            here((chips, rank, depth), bf16),
            here((cols_count, rank_b, depth), f32),
            here((cols_count, rank_b, depth), f32),
            here((3, rows_count, rank_a, part), f32),
            here((3, rows_count, rank_a, part), f32),
            here((rank, part), f32),
            here((rank, part), bf16),
            here((2 * rank, width), bf16),
            here((rank_b, depth), bf16),
            here((cols_count, rank_b, depth), bf16),
            here((2 * rank, depth), f32),
            here((depth, 2 * rank), bf16),
            here((depth, LANES), f32),
            here((blocks, LANES), f32),
            here((cols_count, blocks, LANES), f32),
            dma((fetch_slots,)),
            dma((cols_count + chips + 5,)),
            dma((cols_count + chips + 1,)),
            dma((cols_count + chips + 1,)),
            dma((chips, cols_count + 1)),
            dma((chips, cols_count + 1)),
            dma((2, cols_count)),
            dma((2, cols_count)),
            dma((3, rows_count)),
            dma((3, rows_count)),
            dma((3, rows_count)),
            dma((3, rows_count)),
            dma((rows_count,)),
            dma((rows_count,)),
            dma((2, cols_count)),
            dma((2, cols_count)),
        ],
        compiler_params=pltpu.CompilerParams(
            collective_id=0, has_side_effects=True, vmem_limit_bytes=30_000_000
        ),
    )(
        client_tallies,
        fixed_matrix_encodings,
        line_restore_multiplier.reshape(blocks, LANES),
        central_up_matrix.T,
        running_mean_up.T,
        squared_average_up.T,
        central_down_matrix,
        running_mean_down,
        squared_average_down,
        participant_change_up[0].T,
        participant_change_down[0],
    )
    small = len(small_shapes)
    outs = [pltpu.with_memory_space_constraint(out, pltpu.VMEM) for out in outs]
    normalized, fresh, nb, nmb, nvb, na, nma, nva = pl.pallas_call(
        functools.partial(finish_kernel, small),
        out_shape=[jax.ShapeDtypeStruct((depth, width), bf16)]
        + [jax.ShapeDtypeStruct(shape, f32) for shape in small_shapes],
        in_specs=[vmem] * (2 + small),
        out_specs=[anywhere] * (1 + small),
        scratch_shapes=[
            here((out_slots, out_lines, width), bf16),
            dma((out_slots,)),
            dma((small,)),
        ],
        compiler_params=pltpu.CompilerParams(vmem_limit_bytes=30_000_000),
    )(*outs)
    return (normalized, fresh.reshape(depth), nb.T, na, nmb.T, nvb.T, nma, nva)


def local(*args):
    rows_count, width = lax.axis_size("row"), args[0].shape[1]
    if rows_count % 2 == 0 and width % (rows_count * LANES) == 0:
        return staged_local(*args)
    return direct_local(*args)


def solution(mesh):
    grid = P("row", "col")
    clients = P(("row", "col"), None, None)
    return jax.shard_map(
        local,
        mesh=mesh,
        in_specs=(grid, P("row"), grid, grid, grid, grid, grid, grid, clients, clients, P(("row", "col"), None)),
        out_specs=(grid, P("row"), grid, grid, grid, grid, grid, grid),
        check_vma=False,
    )
```

```python
import functools

import jax
import jax.numpy as jnp
from jax import lax
from jax.experimental import pallas as pl
from jax.experimental.pallas import tpu as pltpu
from jax.sharding import PartitionSpec as P

first_decay = 0.9
second_decay = 0.99
server_rate = 0.1
adam_floor = 0.001
adapter_scale = 2.0
count_scale = 64.0
fp8_top = 448.0
peak_eps = 1e-06
MESH = pl.DeviceIdType.MESH
LANES = 128
decode_lines = 32
merge_lines = 128
code_slots = 3
stage_slots = 2
fetch_lines = 64
fetch_slots = 3
decode_group = 32
decode_width = 1664
pass_width = 512
pass_lines = 32
out_lines = 64
out_slots = 3
decode_plan = (1, 0, 0, 0, 3, 2, 2, 2, 1)


def tile_of(width, limit):
    best = LANES
    for tile in range(LANES, limit + 1, LANES):
        if width % tile == 0:
            best = tile
    return best


def adaptive_update(param, moment, second, grad):
    moment_next = first_decay * moment + (1.0 - first_decay) * grad
    second_next = second_decay * second + (1.0 - second_decay) * grad * grad
    param_next = param - server_rate * moment_next / (jnp.sqrt(second_next) + adam_floor)
    return (param_next, moment_next, second_next)


def scaled_decode(codes):
    low = codes & 127
    mantissa = codes & 7
    mantissa = jnp.where(low > 7, mantissa | 8, mantissa)
    magnitude = mantissa << jnp.maximum(low >> 3, 1)
    return jnp.where(codes > 127, -magnitude, magnitude).astype(jnp.float32)


def merge_kernel(
    rows_count, cols_count,
    codes, scale, pb, mb, vb, pa, ma, va, delta_b, delta_a, weight,
    merged, peak_wide, peak_out, nb, nmb, nvb, na, nma, nva,
    dense, code_buf, got_b, got_a, got_w, fac_b, fac_a, all_b, all_a, wide_b, wide_a,
    left, right, stage, scale_wide, top, top_send, got_top,
    code_sem, out_sem, send_sem, recv_sem, gather_send, gather_recv, own_sem,
):
    my_row, my_col = lax.axis_index("row"), lax.axis_index("col")
    count = rows_count * cols_count
    me = my_row * cols_count + my_col
    depth, width = dense.shape
    steps = depth // decode_lines
    tile = tile_of(width, 1024)
    tiles = width // tile
    rank_b, rank_a = pb.shape[0], pa.shape[0]

    def fetch(i):
        slot = lax.rem(i, code_slots)
        return pltpu.make_async_copy(
            codes.at[pl.ds(i * decode_lines, decode_lines)], code_buf.at[slot], code_sem.at[slot]
        )

    for i in range(code_slots):
        fetch(i).start()

    barrier = pltpu.get_barrier_semaphore()

    def greet(k, _):
        to = lax.rem(me + k, count)
        pl.semaphore_signal(
            barrier, inc=1, device_id=(to // cols_count, lax.rem(to, cols_count)), device_id_type=MESH
        )
        return 0

    lax.fori_loop(1, count, greet, 0)
    pl.semaphore_wait(barrier, count - 1)

    def block_a(row, col):
        return delta_a.at[row, :, pl.ds(pl.multiple_of(col * width, LANES), width)]

    def block_b(row, col):
        return delta_b.at[col, :, pl.ds(pl.multiple_of(row * depth, LANES), depth)]

    def exchange(to, source):
        row, col = to // cols_count, lax.rem(to, cols_count)
        parts = (
            (weight, got_w.at[source]),
            (block_b(row, col), got_b.at[source]),
            (block_a(row, col), got_a.at[source]),
        )
        return [
            pltpu.make_async_remote_copy(
                src_ref=src, dst_ref=dst, send_sem=send_sem.at[n, to], recv_sem=recv_sem.at[n, source],
                device_id=(row, col), device_id_type=MESH,
            )
            for n, (src, dst) in enumerate(parts)
        ]

    def send(k, _):
        for copy in exchange(lax.rem(me + k, count), me):
            copy.start()
        return 0

    lax.fori_loop(1, count, send, 0)
    own = [
        pltpu.make_async_copy(weight, got_w.at[me], own_sem.at[0]),
        pltpu.make_async_copy(block_b(my_row, my_col), got_b.at[me], own_sem.at[1]),
        pltpu.make_async_copy(block_a(my_row, my_col), got_a.at[me], own_sem.at[2]),
    ]
    for copy in own:
        copy.start()

    for b in range(depth // LANES):
        line = jnp.broadcast_to(scale[b : b + 1, :] * 2.0 ** (-10), (LANES, LANES))
        scale_wide[b * LANES : (b + 1) * LANES, :] = line.T

    def decode_step(i, _):
        slot = lax.rem(i, code_slots)
        fetch(i).wait()

        def column(j, _):
            at = pl.ds(pl.multiple_of(j * tile, LANES), tile)
            for g in range(decode_lines // 16):
                value = scaled_decode(code_buf[slot, g * 16 : (g + 1) * 16, at])
                dense[pl.ds(pl.multiple_of(i * decode_lines + g * 16, 16), 16), at] = value.astype(
                    jnp.bfloat16
                )
            return 0

        lax.fori_loop(0, tiles, column, 0)

        @pl.when(i + code_slots < steps)
        def _():
            fetch(i + code_slots).start()

        return 0

    lax.fori_loop(0, steps, decode_step, 0)

    for copy in own:
        copy.wait()

    def arrive(k, _):
        source = lax.rem(me + k, count)
        for copy in exchange(source, source):
            copy.wait_recv()
        return 0

    lax.fori_loop(1, count, arrive, 0)

    def summed(got, which, at, shape):
        def add(s, total):
            return total + got_w[s, which : which + 1, 0:1] * got[s, :, at].astype(jnp.float32)

        return lax.fori_loop(0, count, add, jnp.zeros(shape, jnp.float32), unroll=8)

    grad_b = summed(got_b, 0, slice(None), (rank_b, depth))
    p, m, v = adaptive_update(pb[...], mb[...], vb[...], grad_b)
    nb[...] = p
    nmb[...] = m
    nvb[...] = v
    fac_b[...] = p.astype(jnp.bfloat16)

    def gather_b(to, source):
        return pltpu.make_async_remote_copy(
            src_ref=fac_b, dst_ref=all_b.at[source], send_sem=gather_send.at[0, to],
            recv_sem=gather_recv.at[0, source], device_id=(my_row, to), device_id_type=MESH,
        )

    def gather_a(to, source):
        return pltpu.make_async_remote_copy(
            src_ref=fac_a, dst_ref=all_a.at[source], send_sem=gather_send.at[1, to],
            recv_sem=gather_recv.at[1, source], device_id=(to, my_col), device_id_type=MESH,
        )

    for k in range(1, cols_count):
        gather_b(lax.rem(my_col + k, cols_count), my_col).start()
    own_b = pltpu.make_async_copy(fac_b, all_b.at[my_col], own_sem.at[0])
    own_b.start()

    def update_a(j, _):
        at = pl.ds(pl.multiple_of(j * tile, LANES), tile)
        grad = summed(got_a, 1, at, (rank_a, tile))
        p, m, v = adaptive_update(pa[:, at], ma[:, at], va[:, at], grad)
        na[:, at] = p
        nma[:, at] = m
        nva[:, at] = v
        fac_a[:, at] = p.astype(jnp.bfloat16)
        return 0

    lax.fori_loop(0, tiles, update_a, 0)
    for k in range(1, rows_count):
        gather_a(lax.rem(my_row + k, rows_count), my_row).start()
    own_a = pltpu.make_async_copy(fac_a, all_a.at[my_row], own_sem.at[1])
    own_a.start()

    own_b.wait()
    for k in range(1, cols_count):
        source = lax.rem(my_col + k, cols_count)
        gather_b(source, source).wait_recv()
    for c in range(cols_count):
        wide_b[c * rank_b : (c + 1) * rank_b, :] = all_b[c].astype(jnp.float32)
    left[...] = wide_b[...].T.astype(jnp.bfloat16)

    own_a.wait()
    for k in range(1, rows_count):
        source = lax.rem(my_row + k, rows_count)
        gather_a(source, source).wait_recv()

    def assemble(j, _):
        at = pl.ds(pl.multiple_of(j * tile, LANES), tile)
        for r in range(rows_count):
            wide_a[r * rank_a : (r + 1) * rank_a, :] = all_a[r, :, at].astype(jnp.float32)
        right[:, at] = wide_a[...].astype(jnp.bfloat16)
        return 0

    lax.fori_loop(0, tiles, assemble, 0)

    def put(i):
        slot = lax.rem(i, stage_slots)
        lines = pl.ds(pl.multiple_of(i * merge_lines, merge_lines), merge_lines)
        return pltpu.make_async_copy(stage.at[slot], merged.at[lines], out_sem.at[slot])

    merge_steps = depth // merge_lines

    def merge_step(i, _):
        slot = lax.rem(i, stage_slots)
        lines = pl.ds(pl.multiple_of(i * merge_lines, merge_lines), merge_lines)

        @pl.when(i >= stage_slots)
        def _():
            put(i - stage_slots).wait()

        factor = left[lines, :]
        line_scale = scale_wide[lines, :]

        def column(j, highest):
            for t in range(tile // LANES):
                lane = pl.ds(pl.multiple_of(j * tile + t * LANES, LANES), LANES)
                product = jnp.dot(factor, right[:, lane], preferred_element_type=jnp.float32)
                value = dense[lines, lane].astype(jnp.float32) * line_scale
                value = value + adapter_scale * product
                highest = jnp.maximum(highest, jnp.abs(value))
                stage[slot, :, lane] = value.astype(jnp.bfloat16)
            return highest

        top[lines, :] = lax.fori_loop(
            0, tiles, column, jnp.zeros((merge_lines, LANES), jnp.float32)
        )
        put(i).start()
        return 0

    lax.fori_loop(0, merge_steps, merge_step, 0)

    for b in range(depth // LANES):
        square = top[b * LANES : (b + 1) * LANES, :]
        top_send[b : b + 1, :] = jnp.max(square.T, axis=0, keepdims=True)

    def gather_top(to, source):
        return pltpu.make_async_remote_copy(
            src_ref=top_send, dst_ref=got_top.at[source], send_sem=gather_send.at[2, to],
            recv_sem=gather_recv.at[2, source], device_id=(my_row, to), device_id_type=MESH,
        )

    for k in range(1, cols_count):
        gather_top(lax.rem(my_col + k, cols_count), my_col).start()
    peak = top_send[...]
    for k in range(1, cols_count):
        source = lax.rem(my_col + k, cols_count)
        gather_top(source, source).wait_recv()
        peak = jnp.maximum(peak, got_top[source])
    peak = peak + peak_eps
    peak_out[...] = peak / fp8_top
    for b in range(depth // LANES):
        peak_wide[b * LANES : (b + 1) * LANES, :] = jnp.broadcast_to(
            1.0 / peak[b : b + 1, :], (LANES, LANES)
        ).T

    def drain(i, _):
        put(i).wait()
        return 0

    lax.fori_loop(merge_steps - stage_slots, merge_steps, drain, 0)

    def sent(k, _):
        for copy in exchange(lax.rem(me + k, count), me):
            copy.wait_send()
        return 0

    lax.fori_loop(1, count, sent, 0)
    for k in range(1, cols_count):
        to = lax.rem(my_col + k, cols_count)
        gather_b(to, my_col).wait_send()
        gather_top(to, my_col).wait_send()
    for k in range(1, rows_count):
        gather_a(lax.rem(my_row + k, rows_count), my_row).wait_send()


def normalize_kernel(merged, inverse, out):
    for t in range(merged.shape[1] // LANES):
        at = slice(t * LANES, (t + 1) * LANES)
        out[:, at] = (merged[:, at].astype(jnp.float32) * inverse[...]).astype(jnp.bfloat16)


def direct_local(
    fixed_matrix_encodings,
    line_restore_multiplier,
    central_up_matrix,
    central_down_matrix,
    running_mean_up,
    squared_average_up,
    running_mean_down,
    squared_average_down,
    participant_change_up,
    participant_change_down,
    client_tallies,
):
    rows_count = lax.axis_size("row")
    cols_count = lax.axis_size("col")
    count = rows_count * cols_count
    depth, width = fixed_matrix_encodings.shape
    rank_b = central_up_matrix.shape[1]
    rank_a = central_down_matrix.shape[0]
    rank = participant_change_down.shape[1]
    blocks = depth // LANES
    everyone = client_tallies.shape[0] * count
    weights = client_tallies.astype(jnp.float32) / (count_scale * everyone)
    weight = jnp.broadcast_to(weights[0][:, None], (2, LANES))
    delta_b = participant_change_up[0].T.reshape(cols_count, rank_b, depth * rows_count)
    delta_a = participant_change_down[0].reshape(rows_count, rank_a, width * cols_count)
    anywhere = pl.BlockSpec(memory_space=pl.ANY)
    vmem = pl.BlockSpec(memory_space=pltpu.VMEM)
    f32, bf16 = jnp.float32, jnp.bfloat16
    shape = jax.ShapeDtypeStruct
    outs = pl.pallas_call(
        functools.partial(merge_kernel, rows_count, cols_count),
        out_shape=[
            shape((depth, width), bf16),
            shape((depth, LANES), f32),
            shape((blocks, LANES), f32),
        ]
        + [shape((rank_b, depth), f32)] * 3
        + [shape((rank_a, width), f32)] * 3,
        in_specs=[anywhere] + [vmem] * 7 + [anywhere] * 2 + [vmem],
        out_specs=[anywhere] + [vmem] * 8,
        scratch_shapes=[
            pltpu.VMEM((depth, width), bf16),
            pltpu.VMEM((code_slots, decode_lines, width), jnp.int32),
            pltpu.VMEM((count, rank_b, depth), bf16),
            pltpu.VMEM((count, rank_a, width), bf16),
            pltpu.VMEM((count, 2, LANES), f32),
            pltpu.VMEM((rank_b, depth), bf16),
            pltpu.VMEM((rank_a, width), bf16),
            pltpu.VMEM((cols_count, rank_b, depth), bf16),
            pltpu.VMEM((rows_count, rank_a, width), bf16),
            pltpu.VMEM((rank, depth), f32),
            pltpu.VMEM((rank, tile_of(width, 1024)), f32),
            pltpu.VMEM((depth, rank), bf16),
            pltpu.VMEM((rank, width), bf16),
            pltpu.VMEM((stage_slots, merge_lines, width), bf16),
            pltpu.VMEM((depth, LANES), f32),
            pltpu.VMEM((depth, LANES), f32),
            pltpu.VMEM((blocks, LANES), f32),
            pltpu.VMEM((cols_count, blocks, LANES), f32),
            pltpu.SemaphoreType.DMA((code_slots,)),
            pltpu.SemaphoreType.DMA((stage_slots,)),
            pltpu.SemaphoreType.DMA((3, count)),
            pltpu.SemaphoreType.DMA((3, count)),
            pltpu.SemaphoreType.DMA((3, max(rows_count, cols_count))),
            pltpu.SemaphoreType.DMA((3, max(rows_count, cols_count))),
            pltpu.SemaphoreType.DMA((3,)),
        ],
        compiler_params=pltpu.CompilerParams(
            collective_id=0, has_side_effects=True, vmem_limit_bytes=62_000_000
        ),
    )(
        fixed_matrix_encodings,
        line_restore_multiplier.reshape(blocks, LANES),
        central_up_matrix.T,
        running_mean_up.T,
        squared_average_up.T,
        central_down_matrix,
        running_mean_down,
        squared_average_down,
        delta_b,
        delta_a,
        weight,
    )
    merged, inverse, fresh, nb, nmb, nvb, na, nma, nva = outs
    step = 64
    normalized = pl.pallas_call(
        normalize_kernel,
        grid=(depth // step,),
        out_shape=shape((depth, width), bf16),
        in_specs=[
            pl.BlockSpec((step, width), lambda i: (i, 0)),
            pl.BlockSpec((step, LANES), lambda i: (i, 0)),
        ],
        out_specs=pl.BlockSpec((step, width), lambda i: (i, 0)),
    )(merged, inverse)
    return (normalized, fresh.reshape(depth), nb.T, na, nmb.T, nvb.T, nma, nva)


def packed_decode(codes):
    half = jnp.bfloat16
    value = codes.astype(jnp.float32).astype(half) * half(0.125)
    negative = value > half(15.9)
    value = jnp.where(negative, value - half(16), value)
    power = jnp.floor(jnp.maximum(value, half(1)))
    value = (value - power) + half(1)
    value = jnp.where(negative, -value, value)
    return (value * jnp.exp2(power - half(7))).astype(jnp.float8_e4m3fn)


def staged_kernel(
    rows_count, cols_count, everyone,
    tallies, codes, scale, pb, mb, vb, pa, ma, va, delta_b, delta_a,
    merged, inverse, fresh, nb, nmb, nvb, na, nma, nva,
    dense, code_buf, weight, got_w, mine_a, core_a, pair_a, chip_a, line_a, got_a, sum_a,
    mine_b, core_b, pair_b, chip_b, line_b, got_b,
    state_a, back_a, wide_a, fac_a, right, fac_b, all_b, wide_b, left, top, top_send, got_top,
    code_sem, own_sem, core_send, core_recv, chip_send, chip_recv, line_send, line_recv,
    state_send, state_recv, back_send, back_recv, row_send, row_recv, col_send, col_recv,
):
    my_row, my_col = lax.axis_index("row"), lax.axis_index("col")
    chips = rows_count // 2
    core, chip = lax.rem(my_row, 2), my_row // 2
    depth, width = dense.shape
    rank = delta_a.shape[0]
    rank_b, rank_a = pb.shape[0], pa.shape[0]
    part = width // rows_count
    half = chips * part
    slot_of = core * chips + chip
    tile = tile_of(width, decode_width)
    f32, bf16 = jnp.float32, jnp.bfloat16
    partner = (chip * 2 + 1 - core, my_col)

    def remote(src, dst, send, recv, to):
        return pltpu.make_async_remote_copy(
            src_ref=src, dst_ref=dst, send_sem=send, recv_sem=recv, device_id=to, device_id_type=MESH
        )

    def lanes(start, size):
        return pl.ds(pl.multiple_of(start, LANES), size)

    def fetch(i):
        slot = lax.rem(i, fetch_slots)
        return pltpu.make_async_copy(
            codes.at[pl.ds(i * fetch_lines, fetch_lines)], code_buf.at[slot], code_sem.at[slot]
        )

    steps = depth // fetch_lines
    for i in range(fetch_slots):
        fetch(i).start()

    def own_copies():
        copies = []
        for c in range(cols_count):
            copies.append((delta_a.at[:, lanes(c * width + core * half, half)], mine_a.at[c]))
        for q in range(chips):
            copies.append((delta_b.at[:, lanes((2 * q + core) * depth, depth)], mine_b.at[q]))
        for n, state in enumerate((pa, ma, va)):
            copies.append((state.at[:, lanes(slot_of * part, part)], state_a.at[n, my_row]))
        return [pltpu.make_async_copy(s, d, own_sem.at[n]) for n, (s, d) in enumerate(copies)]

    own = own_copies()
    for copy in own:
        copy.start()

    for n in range(2):
        portion = tallies[0, n].astype(f32) / (count_scale * everyone)
        weight[n * 8 : (n + 1) * 8, :] = jnp.full((8, LANES), portion, f32)

    barrier = pltpu.get_barrier_semaphore()
    for k in range(1, rows_count):
        pl.semaphore_signal(
            barrier, inc=1, device_id=(lax.rem(my_row + k, rows_count), my_col), device_id_type=MESH
        )
    for k in range(1, cols_count):
        pl.semaphore_signal(
            barrier, inc=1, device_id=(my_row, lax.rem(my_col + k, cols_count)), device_id_type=MESH
        )
    pl.semaphore_wait(barrier, rows_count + cols_count - 2)

    def core_copy_a(c):
        return remote(
            delta_a.at[:, lanes(c * width + (1 - core) * half, half)], core_a.at[c],
            core_send.at[c], core_recv.at[c], partner,
        )

    def core_copy_b(q):
        return remote(
            delta_b.at[:, lanes((2 * q + 1 - core) * depth, depth)], core_b.at[q],
            core_send.at[cols_count + q], core_recv.at[cols_count + q], partner,
        )

    last = cols_count + chips
    core_copy_w = remote(weight, got_w, core_send.at[last], core_recv.at[last], partner)

    def state_copy(n, to, source):
        piece = lax.rem(to, 2) * chips + to // 2
        return remote(
            (pa, ma, va)[n].at[:, lanes(piece * part, part)], state_a.at[n, source],
            state_send.at[n, to], state_recv.at[n, source], (to, my_col),
        )

    core_copy_w.start()
    for k in range(1, cols_count + 1):
        core_copy_a(lax.rem(my_col + k, cols_count)).start()
        if k == 1:
            for q in range(chips):
                core_copy_b(q).start()
    for k in range(1, rows_count):
        for n in range(3):
            state_copy(n, lax.rem(my_row + k, rows_count), my_row).start()

    def decode_step(i, _):
        slot = lax.rem(i, fetch_slots)
        fetch(i).wait()

        def column(j, _):
            at = lanes(j * tile, tile)
            for g in range(fetch_lines // decode_group):
                start = pl.multiple_of(i * fetch_lines + g * decode_group, decode_group)
                dense[pl.ds(start, decode_group), at] = packed_decode(
                    code_buf[slot, g * decode_group : (g + 1) * decode_group, at]
                )
            return 0

        lax.fori_loop(0, width // tile, column, 0)

        @pl.when(i + fetch_slots < steps)
        def _():
            fetch(i + fetch_slots).start()

        return 0

    done = [0]
    plan = list(decode_plan)

    def decode_some():
        until = min(steps, done[0] + plan.pop(0)) if plan else steps
        if until > done[0]:
            lax.fori_loop(done[0], until, decode_step, 0)
        done[0] = until

    decode_some()

    for copy in own:
        copy.wait()
    core_copy_w.wait_recv()

    def blend(mine, theirs, which):
        ours = weight[which * 8 : which * 8 + 1, 0:1] * mine.astype(f32)
        return (ours + got_w[which * 8 : which * 8 + 1, 0:1] * theirs.astype(f32)).astype(bf16)

    def chip_copy_a(q, c, source):
        return remote(
            pair_a.at[q, c], chip_a.at[source, c], chip_send.at[q, c], chip_recv.at[source, c],
            (q * 2 + core, my_col),
        )

    def chip_copy_b(q, source):
        return remote(
            pair_b.at[q], chip_b.at[source], chip_send.at[q, cols_count],
            chip_recv.at[source, cols_count], (q * 2 + core, my_col),
        )

    for k in range(1, cols_count + 1):
        c = lax.rem(my_col + k, cols_count)
        core_copy_a(c).wait_recv()
        for q in range(chips):
            at = slice(q * part, (q + 1) * part)
            pair_a[q, c] = blend(mine_a[c, :, at], core_a[c, :, at], 1)
        for j in range(1, chips):
            chip_copy_a(lax.rem(chip + j, chips), c, chip).start()
        if k == 1:
            for q in range(chips):
                core_copy_b(q).wait_recv()
                pair_b[q] = blend(mine_b[q], core_b[q], 0)
            for j in range(1, chips):
                chip_copy_b(lax.rem(chip + j, chips), chip).start()
        decode_some()

    def line_copy_a(c, source):
        return remote(
            line_a.at[c], got_a.at[source], line_send.at[0, c], line_recv.at[0, source], (my_row, c)
        )

    def line_copy_b(c, source):
        return remote(
            line_b.at[c], got_b.at[source], line_send.at[1, c], line_recv.at[1, source], (my_row, c)
        )

    def sum_b():
        total = pair_b[chip].astype(f32)
        for k in range(1, chips):
            source = lax.rem(chip + k, chips)
            chip_copy_b(source, source).wait_recv()
            total = total + chip_b[source].astype(f32)
        for c in range(cols_count):
            line_b[c] = total[c * rank_b : (c + 1) * rank_b, :]
        for k in range(1, cols_count):
            line_copy_b(lax.rem(my_col + k, cols_count), my_col).start()

    for k in range(1, cols_count + 1):
        c = lax.rem(my_col + k, cols_count)
        total = pair_a[chip, c].astype(f32)
        for j in range(1, chips):
            source = lax.rem(chip + j, chips)
            chip_copy_a(source, c, source).wait_recv()
            total = total + chip_a[source, c].astype(f32)
        if k < cols_count:
            line_a[c] = total.astype(bf16)
            line_copy_a(c, my_col).start()
            if k == 1:
                sum_b()
            decode_some()
        else:
            sum_a[...] = total

    decode_some()

    grad = line_b[my_col]
    for k in range(1, cols_count):
        source = lax.rem(my_col + k, cols_count)
        line_copy_b(source, source).wait_recv()
        grad = grad + got_b[source]
    p, m, v = adaptive_update(pb[...], mb[...], vb[...], grad)
    nb[...] = p
    nmb[...] = m
    nvb[...] = v
    fac_b[...] = p.astype(bf16)

    def gather_b(to, source):
        return remote(
            fac_b, all_b.at[source], col_send.at[0, to], col_recv.at[0, source], (my_row, to)
        )

    for k in range(1, cols_count):
        gather_b(lax.rem(my_col + k, cols_count), my_col).start()

    for k in range(1, rows_count):
        for n in range(3):
            source = lax.rem(my_row + k, rows_count)
            state_copy(n, source, source).wait_recv()
    for k in range(1, cols_count):
        source = lax.rem(my_col + k, cols_count)
        line_copy_a(source, source).wait_recv()

    grad = sum_a[...]
    for k in range(1, cols_count):
        grad = grad + got_a[lax.rem(my_col + k, cols_count)].astype(f32)
    for r in range(rows_count):
        at = slice(r * rank_a, (r + 1) * rank_a)
        p, m, v = adaptive_update(state_a[0, r], state_a[1, r], state_a[2, r], grad[at, :])
        back_a[0, r] = p
        back_a[1, r] = m
        back_a[2, r] = v
        wide_a[at, :] = p
    fac_a[...] = wide_a[...].astype(bf16)

    def right_at(row):
        piece = lax.rem(row, 2) * chips + row // 2
        return right.at[0:rank, lanes(piece * part, part)]

    def gather_a(to, source):
        return remote(
            fac_a, right_at(source), row_send.at[to], row_recv.at[source], (to, my_col)
        )

    def back_copy(n, to, source):
        piece = lax.rem(source, 2) * chips + source // 2
        return remote(
            back_a.at[n, to], (na, nma, nva)[n].at[:, lanes(piece * part, part)],
            back_send.at[n, to], back_recv.at[n, source], (to, my_col),
        )

    for j in range(1, chips):
        gather_a(lax.rem(chip + j, chips) * 2 + core, my_row).start()
    for j in range(chips):
        gather_a(lax.rem(chip + j, chips) * 2 + 1 - core, my_row).start()
    own_right = pltpu.make_async_copy(fac_a, right_at(my_row), own_sem.at[0])
    own_right.start()
    own_factor = pltpu.make_async_copy(fac_b, all_b.at[my_col], own_sem.at[1])
    own_factor.start()
    own_back = [
        pltpu.make_async_copy(
            back_a.at[n, my_row], ref.at[:, lanes(slot_of * part, part)], own_sem.at[2 + n]
        )
        for n, ref in enumerate((na, nma, nva))
    ]
    for copy in own_back:
        copy.start()

    plan[:] = []
    decode_some()

    own_factor.wait()
    for k in range(1, cols_count):
        source = lax.rem(my_col + k, cols_count)
        gather_b(source, source).wait_recv()
    for c in range(cols_count):
        wide_b[c * rank_b : (c + 1) * rank_b, :] = all_b[c].astype(f32)
    for b in range(depth // LANES):
        at = slice(b * LANES, (b + 1) * LANES)
        folded = wide_b[0:rank, at] * (adapter_scale / scale[b : b + 1, :])
        high = folded.astype(bf16).astype(f32)
        wide_b[0:rank, at] = high
        wide_b[rank : 2 * rank, at] = folded - high
    left[...] = wide_b[...].T.astype(bf16)

    top[...] = jnp.zeros((depth, LANES), f32)

    def merge_tile(at, size):
        for lines in range(0, depth, 1024):
            deep = min(1024, depth - lines)
            product = jnp.dot(
                left[lines : lines + deep, :], right[:, lanes(at, size)], preferred_element_type=f32
            )
            for g in range(0, deep, pass_lines):
                here = slice(lines + g, lines + g + pass_lines)
                highest = top[here, :]
                for t in range(0, size, LANES):
                    lane = lanes(at + t, LANES)
                    value = product[g : g + pass_lines, t : t + LANES] + dense[here, lane].astype(f32)
                    highest = jnp.maximum(highest, jnp.abs(value))
                    merged[here, lane] = value.astype(bf16)
                top[here, :] = highest

    def merge_piece(row):
        start = (lax.rem(row, 2) * chips + row // 2) * part
        at = lanes(start, part)
        right[rank : 2 * rank, at] = right[0:rank, at]
        whole = part // pass_width

        def column(j, _):
            merge_tile(start + j * pass_width, pass_width)
            return 0

        lax.fori_loop(0, whole, column, 0)
        if part % pass_width:
            merge_tile(start + whole * pass_width, part % pass_width)

    def merge_from(row):
        gather_a(row, row).wait_recv()
        merge_piece(row)

    def near(j, _):
        merge_from(lax.rem(chip + j, chips) * 2 + core)
        return 0

    def far(j, _):
        merge_from(lax.rem(chip + j, chips) * 2 + 1 - core)
        return 0

    own_right.wait()
    merge_piece(my_row)
    lax.fori_loop(1, chips, near, 0)
    for k in range(1, rows_count):
        for n in range(3):
            back_copy(n, lax.rem(my_row + k, rows_count), my_row).start()
    lax.fori_loop(0, chips, far, 0)

    for b in range(depth // LANES):
        square = top[b * LANES : (b + 1) * LANES, :]
        top_send[b : b + 1, :] = jnp.max(square.T, axis=0, keepdims=True)

    def gather_top(to, source):
        return remote(
            top_send, got_top.at[source], col_send.at[1, to], col_recv.at[1, source], (my_row, to)
        )

    for k in range(1, cols_count):
        gather_top(lax.rem(my_col + k, cols_count), my_col).start()
    peak = top_send[...]
    for k in range(1, cols_count):
        source = lax.rem(my_col + k, cols_count)
        gather_top(source, source).wait_recv()
        peak = jnp.maximum(peak, got_top[source])
    peak = peak * scale[...] + peak_eps
    fresh[...] = peak / fp8_top
    ratio = scale[...] / peak
    for b in range(depth // LANES):
        inverse[b * LANES : (b + 1) * LANES, :] = jnp.broadcast_to(
            ratio[b : b + 1, :], (LANES, LANES)
        ).T

    for copy in own_back:
        copy.wait()
    core_copy_w.wait_send()
    for c in range(cols_count):
        core_copy_a(c).wait_send()
    for q in range(chips):
        core_copy_b(q).wait_send()
    for k in range(1, chips):
        q = lax.rem(chip + k, chips)
        chip_copy_b(q, chip).wait_send()
        for c in range(cols_count):
            chip_copy_a(q, c, chip).wait_send()
    for k in range(1, cols_count):
        to = lax.rem(my_col + k, cols_count)
        line_copy_a(to, my_col).wait_send()
        line_copy_b(to, my_col).wait_send()
        gather_b(to, my_col).wait_send()
        gather_top(to, my_col).wait_send()
    for k in range(1, rows_count):
        to = lax.rem(my_row + k, rows_count)
        gather_a(to, my_row).wait_send()
        for n in range(3):
            state_copy(n, to, my_row).wait_send()
            back_copy(n, to, to).wait_recv()
            back_copy(n, to, my_row).wait_send()


def finish_kernel(small, merged, inverse, *refs):
    ins, out, outs = refs[:small], refs[small], refs[small + 1 : 2 * small + 1]
    stage, out_sem, small_sem = refs[2 * small + 1 :]
    depth, width = merged.shape
    tile = tile_of(width, 1024)
    copies = [
        pltpu.make_async_copy(src, dst, small_sem.at[n]) for n, (src, dst) in enumerate(zip(ins, outs))
    ]
    for copy in copies:
        copy.start()

    def put(i):
        slot = lax.rem(i, out_slots)
        return pltpu.make_async_copy(
            stage.at[slot], out.at[pl.ds(pl.multiple_of(i * out_lines, out_lines), out_lines)], out_sem.at[slot]
        )

    steps = depth // out_lines

    def step(i, _):
        slot = lax.rem(i, out_slots)

        @pl.when(i >= out_slots)
        def _():
            put(i - out_slots).wait()

        lines = pl.ds(pl.multiple_of(i * out_lines, out_lines), out_lines)
        factor = inverse[lines, :]

        def column(j, _):
            for t in range(tile // LANES):
                at = pl.ds(pl.multiple_of(j * tile + t * LANES, LANES), LANES)
                stage[slot, :, at] = (merged[lines, at].astype(jnp.float32) * factor).astype(jnp.bfloat16)
            return 0

        lax.fori_loop(0, width // tile, column, 0)
        put(i).start()
        return 0

    lax.fori_loop(0, steps, step, 0)

    def drain(i, _):
        put(i).wait()
        return 0

    lax.fori_loop(steps - out_slots, steps, drain, 0)
    for copy in copies:
        copy.wait()


def staged_local(
    fixed_matrix_encodings,
    line_restore_multiplier,
    central_up_matrix,
    central_down_matrix,
    running_mean_up,
    squared_average_up,
    running_mean_down,
    squared_average_down,
    participant_change_up,
    participant_change_down,
    client_tallies,
):
    rows_count = lax.axis_size("row")
    cols_count = lax.axis_size("col")
    count = rows_count * cols_count
    depth, width = fixed_matrix_encodings.shape
    rank_b = central_up_matrix.shape[1]
    rank_a = central_down_matrix.shape[0]
    rank = participant_change_down.shape[1]
    blocks = depth // LANES
    chips = rows_count // 2
    part = width // rows_count
    half = chips * part
    everyone = client_tallies.shape[0] * count
    anywhere = pl.BlockSpec(memory_space=pl.ANY)
    vmem = pl.BlockSpec(memory_space=pltpu.VMEM)
    f32, bf16 = jnp.float32, jnp.bfloat16
    here = pltpu.VMEM
    dma = pltpu.SemaphoreType.DMA
    small_shapes = [(blocks, LANES)] + [(rank_b, depth)] * 3 + [(rank_a, width)] * 3
    outs = pl.pallas_call(
        functools.partial(staged_kernel, rows_count, cols_count, everyone),
        out_shape=[here((depth, width), bf16), here((depth, LANES), f32)]
        + [here(shape, f32) for shape in small_shapes],
        in_specs=[pl.BlockSpec(memory_space=pltpu.SMEM), anywhere] + [vmem] * 7 + [anywhere] * 2,
        out_specs=[vmem] * 9,
        scratch_shapes=[
            here((depth, width), jnp.float8_e4m3fn),
            here((fetch_slots, fetch_lines, width), jnp.int32),
            here((16, LANES), f32),
            here((16, LANES), f32),
            here((cols_count, rank, half), bf16),
            here((cols_count, rank, half), bf16),
            here((chips, cols_count, rank, part), bf16),
            here((chips, cols_count, rank, part), bf16),
            here((cols_count, rank, part), bf16),
            here((cols_count, rank, part), bf16),
            here((rank, part), f32),
            here((chips, rank, depth), bf16),
            here((chips, rank, depth), bf16),
            here((chips, rank, depth), bf16),
            here((chips, rank, depth), bf16),
            here((cols_count, rank_b, depth), f32),
            here((cols_count, rank_b, depth), f32),
            here((3, rows_count, rank_a, part), f32),
            here((3, rows_count, rank_a, part), f32),
            here((rank, part), f32),
            here((rank, part), bf16),
            here((2 * rank, width), bf16),
            here((rank_b, depth), bf16),
            here((cols_count, rank_b, depth), bf16),
            here((2 * rank, depth), f32),
            here((depth, 2 * rank), bf16),
            here((depth, LANES), f32),
            here((blocks, LANES), f32),
            here((cols_count, blocks, LANES), f32),
            dma((fetch_slots,)),
            dma((cols_count + chips + 5,)),
            dma((cols_count + chips + 1,)),
            dma((cols_count + chips + 1,)),
            dma((chips, cols_count + 1)),
            dma((chips, cols_count + 1)),
            dma((2, cols_count)),
            dma((2, cols_count)),
            dma((3, rows_count)),
            dma((3, rows_count)),
            dma((3, rows_count)),
            dma((3, rows_count)),
            dma((rows_count,)),
            dma((rows_count,)),
            dma((2, cols_count)),
            dma((2, cols_count)),
        ],
        compiler_params=pltpu.CompilerParams(
            collective_id=0, has_side_effects=True, vmem_limit_bytes=38_000_000
        ),
    )(
        client_tallies,
        fixed_matrix_encodings,
        line_restore_multiplier.reshape(blocks, LANES),
        central_up_matrix.T,
        running_mean_up.T,
        squared_average_up.T,
        central_down_matrix,
        running_mean_down,
        squared_average_down,
        participant_change_up[0].T,
        participant_change_down[0],
    )
    small = len(small_shapes)
    outs = [pltpu.with_memory_space_constraint(out, pltpu.VMEM) for out in outs]
    normalized, fresh, nb, nmb, nvb, na, nma, nva = pl.pallas_call(
        functools.partial(finish_kernel, small),
        out_shape=[jax.ShapeDtypeStruct((depth, width), bf16)]
        + [jax.ShapeDtypeStruct(shape, f32) for shape in small_shapes],
        in_specs=[vmem] * (2 + small),
        out_specs=[anywhere] * (1 + small),
        scratch_shapes=[
            here((out_slots, out_lines, width), bf16),
            dma((out_slots,)),
            dma((small,)),
        ],
        compiler_params=pltpu.CompilerParams(vmem_limit_bytes=38_000_000),
    )(*outs)
    return (normalized, fresh.reshape(depth), nb.T, na, nmb.T, nvb.T, nma, nva)


def local(*args):
    rows_count, width = lax.axis_size("row"), args[0].shape[1]
    if rows_count % 2 == 0 and width % (rows_count * LANES) == 0:
        return staged_local(*args)
    return direct_local(*args)


def solution(mesh):
    grid = P("row", "col")
    clients = P(("row", "col"), None, None)
    return jax.shard_map(
        local,
        mesh=mesh,
        in_specs=(grid, P("row"), grid, grid, grid, grid, grid, grid, clients, clients, P(("row", "col"), None)),
        out_specs=(grid, P("row"), grid, grid, grid, grid, grid, grid),
        check_vma=False,
    )
```

```python
import functools

import jax
import jax.numpy as jnp
from jax import lax
from jax.experimental import pallas as pl
from jax.experimental.pallas import tpu as pltpu
from jax.sharding import PartitionSpec as P

first_decay = 0.9
second_decay = 0.99
server_rate = 0.1
adam_floor = 0.001
adapter_scale = 2.0
count_scale = 64.0
fp8_top = 448.0
peak_eps = 1e-06
MESH = pl.DeviceIdType.MESH
LANES = 128
decode_lines = 32
merge_lines = 128
code_slots = 3
stage_slots = 2
fetch_lines = 64
fetch_slots = 3
decode_group = 32
decode_width = 1664
pass_width = 512
pass_lines = 32
out_lines = 64
out_slots = 3
decode_plan = (2, 0, 0, 0, 8, 4, 4, 4, 4)


def tile_of(width, limit):
    best = LANES
    for tile in range(LANES, limit + 1, LANES):
        if width % tile == 0:
            best = tile
    return best


def adaptive_update(param, moment, second, grad):
    moment_next = first_decay * moment + (1.0 - first_decay) * grad
    second_next = second_decay * second + (1.0 - second_decay) * grad * grad
    param_next = param - server_rate * moment_next / (jnp.sqrt(second_next) + adam_floor)
    return (param_next, moment_next, second_next)


def scaled_decode(codes):
    low = codes & 127
    mantissa = codes & 7
    mantissa = jnp.where(low > 7, mantissa | 8, mantissa)
    magnitude = mantissa << jnp.maximum(low >> 3, 1)
    return jnp.where(codes > 127, -magnitude, magnitude).astype(jnp.float32)


def merge_kernel(
    rows_count, cols_count,
    codes, scale, pb, mb, vb, pa, ma, va, delta_b, delta_a, weight,
    merged, peak_wide, peak_out, nb, nmb, nvb, na, nma, nva,
    dense, code_buf, got_b, got_a, got_w, fac_b, fac_a, all_b, all_a, wide_b, wide_a,
    left, right, stage, scale_wide, top, top_send, got_top,
    code_sem, out_sem, send_sem, recv_sem, gather_send, gather_recv, own_sem,
):
    my_row, my_col = lax.axis_index("row"), lax.axis_index("col")
    count = rows_count * cols_count
    me = my_row * cols_count + my_col
    depth, width = dense.shape
    steps = depth // decode_lines
    tile = tile_of(width, 1024)
    tiles = width // tile
    rank_b, rank_a = pb.shape[0], pa.shape[0]

    def fetch(i):
        slot = lax.rem(i, code_slots)
        return pltpu.make_async_copy(
            codes.at[pl.ds(i * decode_lines, decode_lines)], code_buf.at[slot], code_sem.at[slot]
        )

    for i in range(code_slots):
        fetch(i).start()

    barrier = pltpu.get_barrier_semaphore()

    def greet(k, _):
        to = lax.rem(me + k, count)
        pl.semaphore_signal(
            barrier, inc=1, device_id=(to // cols_count, lax.rem(to, cols_count)), device_id_type=MESH
        )
        return 0

    lax.fori_loop(1, count, greet, 0)
    pl.semaphore_wait(barrier, count - 1)

    def block_a(row, col):
        return delta_a.at[row, :, pl.ds(pl.multiple_of(col * width, LANES), width)]

    def block_b(row, col):
        return delta_b.at[col, :, pl.ds(pl.multiple_of(row * depth, LANES), depth)]

    def exchange(to, source):
        row, col = to // cols_count, lax.rem(to, cols_count)
        parts = (
            (weight, got_w.at[source]),
            (block_b(row, col), got_b.at[source]),
            (block_a(row, col), got_a.at[source]),
        )
        return [
            pltpu.make_async_remote_copy(
                src_ref=src, dst_ref=dst, send_sem=send_sem.at[n, to], recv_sem=recv_sem.at[n, source],
                device_id=(row, col), device_id_type=MESH,
            )
            for n, (src, dst) in enumerate(parts)
        ]

    def send(k, _):
        for copy in exchange(lax.rem(me + k, count), me):
            copy.start()
        return 0

    lax.fori_loop(1, count, send, 0)
    own = [
        pltpu.make_async_copy(weight, got_w.at[me], own_sem.at[0]),
        pltpu.make_async_copy(block_b(my_row, my_col), got_b.at[me], own_sem.at[1]),
        pltpu.make_async_copy(block_a(my_row, my_col), got_a.at[me], own_sem.at[2]),
    ]
    for copy in own:
        copy.start()

    for b in range(depth // LANES):
        line = jnp.broadcast_to(scale[b : b + 1, :] * 2.0 ** (-10), (LANES, LANES))
        scale_wide[b * LANES : (b + 1) * LANES, :] = line.T

    def decode_step(i, _):
        slot = lax.rem(i, code_slots)
        fetch(i).wait()

        def column(j, _):
            at = pl.ds(pl.multiple_of(j * tile, LANES), tile)
            for g in range(decode_lines // 16):
                value = scaled_decode(code_buf[slot, g * 16 : (g + 1) * 16, at])
                dense[pl.ds(pl.multiple_of(i * decode_lines + g * 16, 16), 16), at] = value.astype(
                    jnp.bfloat16
                )
            return 0

        lax.fori_loop(0, tiles, column, 0)

        @pl.when(i + code_slots < steps)
        def _():
            fetch(i + code_slots).start()

        return 0

    lax.fori_loop(0, steps, decode_step, 0)

    for copy in own:
        copy.wait()

    def arrive(k, _):
        source = lax.rem(me + k, count)
        for copy in exchange(source, source):
            copy.wait_recv()
        return 0

    lax.fori_loop(1, count, arrive, 0)

    def summed(got, which, at, shape):
        def add(s, total):
            return total + got_w[s, which : which + 1, 0:1] * got[s, :, at].astype(jnp.float32)

        return lax.fori_loop(0, count, add, jnp.zeros(shape, jnp.float32), unroll=8)

    grad_b = summed(got_b, 0, slice(None), (rank_b, depth))
    p, m, v = adaptive_update(pb[...], mb[...], vb[...], grad_b)
    nb[...] = p
    nmb[...] = m
    nvb[...] = v
    fac_b[...] = p.astype(jnp.bfloat16)

    def gather_b(to, source):
        return pltpu.make_async_remote_copy(
            src_ref=fac_b, dst_ref=all_b.at[source], send_sem=gather_send.at[0, to],
            recv_sem=gather_recv.at[0, source], device_id=(my_row, to), device_id_type=MESH,
        )

    def gather_a(to, source):
        return pltpu.make_async_remote_copy(
            src_ref=fac_a, dst_ref=all_a.at[source], send_sem=gather_send.at[1, to],
            recv_sem=gather_recv.at[1, source], device_id=(to, my_col), device_id_type=MESH,
        )

    for k in range(1, cols_count):
        gather_b(lax.rem(my_col + k, cols_count), my_col).start()
    own_b = pltpu.make_async_copy(fac_b, all_b.at[my_col], own_sem.at[0])
    own_b.start()

    def update_a(j, _):
        at = pl.ds(pl.multiple_of(j * tile, LANES), tile)
        grad = summed(got_a, 1, at, (rank_a, tile))
        p, m, v = adaptive_update(pa[:, at], ma[:, at], va[:, at], grad)
        na[:, at] = p
        nma[:, at] = m
        nva[:, at] = v
        fac_a[:, at] = p.astype(jnp.bfloat16)
        return 0

    lax.fori_loop(0, tiles, update_a, 0)
    for k in range(1, rows_count):
        gather_a(lax.rem(my_row + k, rows_count), my_row).start()
    own_a = pltpu.make_async_copy(fac_a, all_a.at[my_row], own_sem.at[1])
    own_a.start()

    own_b.wait()
    for k in range(1, cols_count):
        source = lax.rem(my_col + k, cols_count)
        gather_b(source, source).wait_recv()
    for c in range(cols_count):
        wide_b[c * rank_b : (c + 1) * rank_b, :] = all_b[c].astype(jnp.float32)
    left[...] = wide_b[...].T.astype(jnp.bfloat16)

    own_a.wait()
    for k in range(1, rows_count):
        source = lax.rem(my_row + k, rows_count)
        gather_a(source, source).wait_recv()

    def assemble(j, _):
        at = pl.ds(pl.multiple_of(j * tile, LANES), tile)
        for r in range(rows_count):
            wide_a[r * rank_a : (r + 1) * rank_a, :] = all_a[r, :, at].astype(jnp.float32)
        right[:, at] = wide_a[...].astype(jnp.bfloat16)
        return 0

    lax.fori_loop(0, tiles, assemble, 0)

    def put(i):
        slot = lax.rem(i, stage_slots)
        lines = pl.ds(pl.multiple_of(i * merge_lines, merge_lines), merge_lines)
        return pltpu.make_async_copy(stage.at[slot], merged.at[lines], out_sem.at[slot])

    merge_steps = depth // merge_lines

    def merge_step(i, _):
        slot = lax.rem(i, stage_slots)
        lines = pl.ds(pl.multiple_of(i * merge_lines, merge_lines), merge_lines)

        @pl.when(i >= stage_slots)
        def _():
            put(i - stage_slots).wait()

        factor = left[lines, :]
        line_scale = scale_wide[lines, :]

        def column(j, highest):
            for t in range(tile // LANES):
                lane = pl.ds(pl.multiple_of(j * tile + t * LANES, LANES), LANES)
                product = jnp.dot(factor, right[:, lane], preferred_element_type=jnp.float32)
                value = dense[lines, lane].astype(jnp.float32) * line_scale
                value = value + adapter_scale * product
                highest = jnp.maximum(highest, jnp.abs(value))
                stage[slot, :, lane] = value.astype(jnp.bfloat16)
            return highest

        top[lines, :] = lax.fori_loop(
            0, tiles, column, jnp.zeros((merge_lines, LANES), jnp.float32)
        )
        put(i).start()
        return 0

    lax.fori_loop(0, merge_steps, merge_step, 0)

    for b in range(depth // LANES):
        square = top[b * LANES : (b + 1) * LANES, :]
        top_send[b : b + 1, :] = jnp.max(square.T, axis=0, keepdims=True)

    def gather_top(to, source):
        return pltpu.make_async_remote_copy(
            src_ref=top_send, dst_ref=got_top.at[source], send_sem=gather_send.at[2, to],
            recv_sem=gather_recv.at[2, source], device_id=(my_row, to), device_id_type=MESH,
        )

    for k in range(1, cols_count):
        gather_top(lax.rem(my_col + k, cols_count), my_col).start()
    peak = top_send[...]
    for k in range(1, cols_count):
        source = lax.rem(my_col + k, cols_count)
        gather_top(source, source).wait_recv()
        peak = jnp.maximum(peak, got_top[source])
    peak = peak + peak_eps
    peak_out[...] = peak / fp8_top
    for b in range(depth // LANES):
        peak_wide[b * LANES : (b + 1) * LANES, :] = jnp.broadcast_to(
            1.0 / peak[b : b + 1, :], (LANES, LANES)
        ).T

    def drain(i, _):
        put(i).wait()
        return 0

    lax.fori_loop(merge_steps - stage_slots, merge_steps, drain, 0)

    def sent(k, _):
        for copy in exchange(lax.rem(me + k, count), me):
            copy.wait_send()
        return 0

    lax.fori_loop(1, count, sent, 0)
    for k in range(1, cols_count):
        to = lax.rem(my_col + k, cols_count)
        gather_b(to, my_col).wait_send()
        gather_top(to, my_col).wait_send()
    for k in range(1, rows_count):
        gather_a(lax.rem(my_row + k, rows_count), my_row).wait_send()


def normalize_kernel(merged, inverse, out):
    for t in range(merged.shape[1] // LANES):
        at = slice(t * LANES, (t + 1) * LANES)
        out[:, at] = (merged[:, at].astype(jnp.float32) * inverse[...]).astype(jnp.bfloat16)


def direct_local(
    fixed_matrix_encodings,
    line_restore_multiplier,
    central_up_matrix,
    central_down_matrix,
    running_mean_up,
    squared_average_up,
    running_mean_down,
    squared_average_down,
    participant_change_up,
    participant_change_down,
    client_tallies,
):
    rows_count = lax.axis_size("row")
    cols_count = lax.axis_size("col")
    count = rows_count * cols_count
    depth, width = fixed_matrix_encodings.shape
    rank_b = central_up_matrix.shape[1]
    rank_a = central_down_matrix.shape[0]
    rank = participant_change_down.shape[1]
    blocks = depth // LANES
    everyone = client_tallies.shape[0] * count
    weights = client_tallies.astype(jnp.float32) / (count_scale * everyone)
    weight = jnp.broadcast_to(weights[0][:, None], (2, LANES))
    delta_b = participant_change_up[0].T.reshape(cols_count, rank_b, depth * rows_count)
    delta_a = participant_change_down[0].reshape(rows_count, rank_a, width * cols_count)
    anywhere = pl.BlockSpec(memory_space=pl.ANY)
    vmem = pl.BlockSpec(memory_space=pltpu.VMEM)
    f32, bf16 = jnp.float32, jnp.bfloat16
    shape = jax.ShapeDtypeStruct
    outs = pl.pallas_call(
        functools.partial(merge_kernel, rows_count, cols_count),
        out_shape=[
            shape((depth, width), bf16),
            shape((depth, LANES), f32),
            shape((blocks, LANES), f32),
        ]
        + [shape((rank_b, depth), f32)] * 3
        + [shape((rank_a, width), f32)] * 3,
        in_specs=[anywhere] + [vmem] * 7 + [anywhere] * 2 + [vmem],
        out_specs=[anywhere] + [vmem] * 8,
        scratch_shapes=[
            pltpu.VMEM((depth, width), bf16),
            pltpu.VMEM((code_slots, decode_lines, width), jnp.int32),
            pltpu.VMEM((count, rank_b, depth), bf16),
            pltpu.VMEM((count, rank_a, width), bf16),
            pltpu.VMEM((count, 2, LANES), f32),
            pltpu.VMEM((rank_b, depth), bf16),
            pltpu.VMEM((rank_a, width), bf16),
            pltpu.VMEM((cols_count, rank_b, depth), bf16),
            pltpu.VMEM((rows_count, rank_a, width), bf16),
            pltpu.VMEM((rank, depth), f32),
            pltpu.VMEM((rank, tile_of(width, 1024)), f32),
            pltpu.VMEM((depth, rank), bf16),
            pltpu.VMEM((rank, width), bf16),
            pltpu.VMEM((stage_slots, merge_lines, width), bf16),
            pltpu.VMEM((depth, LANES), f32),
            pltpu.VMEM((depth, LANES), f32),
            pltpu.VMEM((blocks, LANES), f32),
            pltpu.VMEM((cols_count, blocks, LANES), f32),
            pltpu.SemaphoreType.DMA((code_slots,)),
            pltpu.SemaphoreType.DMA((stage_slots,)),
            pltpu.SemaphoreType.DMA((3, count)),
            pltpu.SemaphoreType.DMA((3, count)),
            pltpu.SemaphoreType.DMA((3, max(rows_count, cols_count))),
            pltpu.SemaphoreType.DMA((3, max(rows_count, cols_count))),
            pltpu.SemaphoreType.DMA((3,)),
        ],
        compiler_params=pltpu.CompilerParams(
            collective_id=0, has_side_effects=True, vmem_limit_bytes=62_000_000
        ),
    )(
        fixed_matrix_encodings,
        line_restore_multiplier.reshape(blocks, LANES),
        central_up_matrix.T,
        running_mean_up.T,
        squared_average_up.T,
        central_down_matrix,
        running_mean_down,
        squared_average_down,
        delta_b,
        delta_a,
        weight,
    )
    merged, inverse, fresh, nb, nmb, nvb, na, nma, nva = outs
    step = 64
    normalized = pl.pallas_call(
        normalize_kernel,
        grid=(depth // step,),
        out_shape=shape((depth, width), bf16),
        in_specs=[
            pl.BlockSpec((step, width), lambda i: (i, 0)),
            pl.BlockSpec((step, LANES), lambda i: (i, 0)),
        ],
        out_specs=pl.BlockSpec((step, width), lambda i: (i, 0)),
    )(merged, inverse)
    return (normalized, fresh.reshape(depth), nb.T, na, nmb.T, nvb.T, nma, nva)


def packed_decode(codes):
    half = jnp.bfloat16
    value = codes.astype(jnp.float32).astype(half) * half(0.125)
    negative = value > half(15.9)
    value = jnp.where(negative, value - half(16), value)
    power = jnp.floor(jnp.maximum(value, half(1)))
    value = (value - power) + half(1)
    value = jnp.where(negative, -value, value)
    return (value * jnp.exp2(power - half(7))).astype(jnp.float8_e4m3fn)


def staged_kernel(
    rows_count, cols_count, everyone,
    tallies, codes, scale, pb, mb, vb, pa, ma, va, delta_b, delta_a,
    merged, inverse, fresh, nb, nmb, nvb, na, nma, nva,
    dense, code_buf, weight, got_w, mine_a, core_a, pair_a, chip_a, line_a, got_a, sum_a,
    mine_b, core_b, pair_b, chip_b, line_b, got_b,
    state_a, back_a, wide_a, fac_a, right, fac_b, all_b, wide_b, left, top, top_send, got_top,
    code_sem, own_sem, core_send, core_recv, chip_send, chip_recv, line_send, line_recv,
    state_send, state_recv, back_send, back_recv, row_send, row_recv, col_send, col_recv,
):
    my_row, my_col = lax.axis_index("row"), lax.axis_index("col")
    chips = rows_count // 2
    core, chip = lax.rem(my_row, 2), my_row // 2
    depth, width = dense.shape
    rank = delta_a.shape[0]
    rank_b, rank_a = pb.shape[0], pa.shape[0]
    part = width // rows_count
    half = chips * part
    slot_of = core * chips + chip
    tile = tile_of(width, decode_width)
    f32, bf16 = jnp.float32, jnp.bfloat16
    partner = (chip * 2 + 1 - core, my_col)

    def remote(src, dst, send, recv, to):
        return pltpu.make_async_remote_copy(
            src_ref=src, dst_ref=dst, send_sem=send, recv_sem=recv, device_id=to, device_id_type=MESH
        )

    def lanes(start, size):
        return pl.ds(pl.multiple_of(start, LANES), size)

    def fetch(i):
        slot = lax.rem(i, fetch_slots)
        return pltpu.make_async_copy(
            codes.at[pl.ds(i * fetch_lines, fetch_lines)], code_buf.at[slot], code_sem.at[slot]
        )

    steps = depth // fetch_lines
    for i in range(fetch_slots):
        fetch(i).start()

    def own_copies():
        copies = []
        for c in range(cols_count):
            copies.append((delta_a.at[:, lanes(c * width + core * half, half)], mine_a.at[c]))
        for q in range(chips):
            copies.append((delta_b.at[:, lanes((2 * q + core) * depth, depth)], mine_b.at[q]))
        for n, state in enumerate((pa, ma, va)):
            copies.append((state.at[:, lanes(slot_of * part, part)], state_a.at[n, my_row]))
        return [pltpu.make_async_copy(s, d, own_sem.at[n]) for n, (s, d) in enumerate(copies)]

    own = own_copies()
    for copy in own:
        copy.start()

    for n in range(2):
        portion = tallies[0, n].astype(f32) / (count_scale * everyone)
        weight[n * 8 : (n + 1) * 8, :] = jnp.full((8, LANES), portion, f32)

    barrier = pltpu.get_barrier_semaphore()
    for k in range(1, rows_count):
        pl.semaphore_signal(
            barrier, inc=1, device_id=(lax.rem(my_row + k, rows_count), my_col), device_id_type=MESH
        )
    for k in range(1, cols_count):
        pl.semaphore_signal(
            barrier, inc=1, device_id=(my_row, lax.rem(my_col + k, cols_count)), device_id_type=MESH
        )
    pl.semaphore_wait(barrier, rows_count + cols_count - 2)

    def core_copy_a(c):
        return remote(
            delta_a.at[:, lanes(c * width + (1 - core) * half, half)], core_a.at[c],
            core_send.at[c], core_recv.at[c], partner,
        )

    def core_copy_b(q):
        return remote(
            delta_b.at[:, lanes((2 * q + 1 - core) * depth, depth)], core_b.at[q],
            core_send.at[cols_count + q], core_recv.at[cols_count + q], partner,
        )

    last = cols_count + chips
    core_copy_w = remote(weight, got_w, core_send.at[last], core_recv.at[last], partner)

    def state_copy(n, to, source):
        piece = lax.rem(to, 2) * chips + to // 2
        return remote(
            (pa, ma, va)[n].at[:, lanes(piece * part, part)], state_a.at[n, source],
            state_send.at[n, to], state_recv.at[n, source], (to, my_col),
        )

    core_copy_w.start()
    for k in range(1, cols_count + 1):
        core_copy_a(lax.rem(my_col + k, cols_count)).start()
        if k == 1:
            for q in range(chips):
                core_copy_b(q).start()
    for k in range(1, rows_count):
        for n in range(3):
            state_copy(n, lax.rem(my_row + k, rows_count), my_row).start()

    splits = 2 if width // tile % 2 == 0 else 1
    share = width // tile // splits

    def decode_step(unit, _):
        i, turn = unit // splits, lax.rem(unit, splits)
        slot = lax.rem(i, fetch_slots)

        @pl.when(turn == 0)
        def _():
            fetch(i).wait()

        def column(j, _):
            at = lanes((turn * share + j) * tile, tile)
            for g in range(fetch_lines // decode_group):
                start = pl.multiple_of(i * fetch_lines + g * decode_group, decode_group)
                dense[pl.ds(start, decode_group), at] = packed_decode(
                    code_buf[slot, g * decode_group : (g + 1) * decode_group, at]
                )
            return 0

        lax.fori_loop(0, share, column, 0)

        @pl.when((i + fetch_slots < steps) & (turn == splits - 1))
        def _():
            fetch(i + fetch_slots).start()

        return 0

    done = [0]
    plan = list(decode_plan)
    units = steps * splits

    def decode_some():
        until = min(units, done[0] + plan.pop(0)) if plan else units
        if until > done[0]:
            lax.fori_loop(done[0], until, decode_step, 0)
        done[0] = until

    decode_some()

    for copy in own:
        copy.wait()
    core_copy_w.wait_recv()

    def blend(mine, theirs, which):
        ours = weight[which * 8 : which * 8 + 1, 0:1] * mine.astype(f32)
        return (ours + got_w[which * 8 : which * 8 + 1, 0:1] * theirs.astype(f32)).astype(bf16)

    def chip_copy_a(q, c, source):
        return remote(
            pair_a.at[q, c], chip_a.at[source, c], chip_send.at[q, c], chip_recv.at[source, c],
            (q * 2 + core, my_col),
        )

    def chip_copy_b(q, source):
        return remote(
            pair_b.at[q], chip_b.at[source], chip_send.at[q, cols_count],
            chip_recv.at[source, cols_count], (q * 2 + core, my_col),
        )

    for k in range(1, cols_count + 1):
        c = lax.rem(my_col + k, cols_count)
        core_copy_a(c).wait_recv()
        for q in range(chips):
            at = slice(q * part, (q + 1) * part)
            pair_a[q, c] = blend(mine_a[c, :, at], core_a[c, :, at], 1)
        for j in range(1, chips):
            chip_copy_a(lax.rem(chip + j, chips), c, chip).start()
        if k == 1:
            for q in range(chips):
                core_copy_b(q).wait_recv()
                pair_b[q] = blend(mine_b[q], core_b[q], 0)
            for j in range(1, chips):
                chip_copy_b(lax.rem(chip + j, chips), chip).start()
        decode_some()

    def line_copy_a(c, source):
        return remote(
            line_a.at[c], got_a.at[source], line_send.at[0, c], line_recv.at[0, source], (my_row, c)
        )

    def line_copy_b(c, source):
        return remote(
            line_b.at[c], got_b.at[source], line_send.at[1, c], line_recv.at[1, source], (my_row, c)
        )

    def sum_b():
        total = pair_b[chip].astype(f32)
        for k in range(1, chips):
            source = lax.rem(chip + k, chips)
            chip_copy_b(source, source).wait_recv()
            total = total + chip_b[source].astype(f32)
        for c in range(cols_count):
            line_b[c] = total[c * rank_b : (c + 1) * rank_b, :]
        for k in range(1, cols_count):
            line_copy_b(lax.rem(my_col + k, cols_count), my_col).start()

    for k in range(1, cols_count + 1):
        c = lax.rem(my_col + k, cols_count)
        total = pair_a[chip, c].astype(f32)
        for j in range(1, chips):
            source = lax.rem(chip + j, chips)
            chip_copy_a(source, c, source).wait_recv()
            total = total + chip_a[source, c].astype(f32)
        if k < cols_count:
            line_a[c] = total.astype(bf16)
            line_copy_a(c, my_col).start()
            if k == 1:
                sum_b()
            decode_some()
        else:
            sum_a[...] = total

    decode_some()

    grad = line_b[my_col]
    for k in range(1, cols_count):
        source = lax.rem(my_col + k, cols_count)
        line_copy_b(source, source).wait_recv()
        grad = grad + got_b[source]
    p, m, v = adaptive_update(pb[...], mb[...], vb[...], grad)
    nb[...] = p
    nmb[...] = m
    nvb[...] = v
    fac_b[...] = p.astype(bf16)

    def gather_b(to, source):
        return remote(
            fac_b, all_b.at[source], col_send.at[0, to], col_recv.at[0, source], (my_row, to)
        )

    for k in range(1, cols_count):
        gather_b(lax.rem(my_col + k, cols_count), my_col).start()

    for k in range(1, rows_count):
        for n in range(3):
            source = lax.rem(my_row + k, rows_count)
            state_copy(n, source, source).wait_recv()
    for k in range(1, cols_count):
        source = lax.rem(my_col + k, cols_count)
        line_copy_a(source, source).wait_recv()

    grad = sum_a[...]
    for k in range(1, cols_count):
        grad = grad + got_a[lax.rem(my_col + k, cols_count)].astype(f32)
    for r in range(rows_count):
        at = slice(r * rank_a, (r + 1) * rank_a)
        p, m, v = adaptive_update(state_a[0, r], state_a[1, r], state_a[2, r], grad[at, :])
        back_a[0, r] = p
        back_a[1, r] = m
        back_a[2, r] = v
        wide_a[at, :] = p
    fac_a[...] = wide_a[...].astype(bf16)

    def right_at(row):
        piece = lax.rem(row, 2) * chips + row // 2
        return right.at[0:rank, lanes(piece * part, part)]

    def gather_a(to, source):
        return remote(
            fac_a, right_at(source), row_send.at[to], row_recv.at[source], (to, my_col)
        )

    def back_copy(n, to, source):
        piece = lax.rem(source, 2) * chips + source // 2
        return remote(
            back_a.at[n, to], (na, nma, nva)[n].at[:, lanes(piece * part, part)],
            back_send.at[n, to], back_recv.at[n, source], (to, my_col),
        )

    for j in range(1, chips):
        gather_a(lax.rem(chip + j, chips) * 2 + core, my_row).start()
    for j in range(chips):
        gather_a(lax.rem(chip + j, chips) * 2 + 1 - core, my_row).start()
    own_right = pltpu.make_async_copy(fac_a, right_at(my_row), own_sem.at[0])
    own_right.start()
    own_factor = pltpu.make_async_copy(fac_b, all_b.at[my_col], own_sem.at[1])
    own_factor.start()
    own_back = [
        pltpu.make_async_copy(
            back_a.at[n, my_row], ref.at[:, lanes(slot_of * part, part)], own_sem.at[2 + n]
        )
        for n, ref in enumerate((na, nma, nva))
    ]
    for copy in own_back:
        copy.start()

    plan[:] = []
    decode_some()

    own_factor.wait()
    for k in range(1, cols_count):
        source = lax.rem(my_col + k, cols_count)
        gather_b(source, source).wait_recv()
    for c in range(cols_count):
        wide_b[c * rank_b : (c + 1) * rank_b, :] = all_b[c].astype(f32)
    for b in range(depth // LANES):
        at = slice(b * LANES, (b + 1) * LANES)
        folded = wide_b[0:rank, at] * (adapter_scale / scale[b : b + 1, :])
        high = folded.astype(bf16).astype(f32)
        wide_b[0:rank, at] = high
        wide_b[rank : 2 * rank, at] = folded - high
    left[...] = wide_b[...].T.astype(bf16)

    top[...] = jnp.zeros((depth, LANES), f32)

    def merge_tile(at, size):
        for lines in range(0, depth, 1024):
            deep = min(1024, depth - lines)
            product = jnp.dot(
                left[lines : lines + deep, :], right[:, lanes(at, size)], preferred_element_type=f32
            )
            for g in range(0, deep, pass_lines):
                here = slice(lines + g, lines + g + pass_lines)
                highest = top[here, :]
                for t in range(0, size, LANES):
                    lane = lanes(at + t, LANES)
                    value = product[g : g + pass_lines, t : t + LANES] + dense[here, lane].astype(f32)
                    highest = jnp.maximum(highest, jnp.abs(value))
                    merged[here, lane] = value.astype(bf16)
                top[here, :] = highest

    def merge_piece(start, size):
        at = lanes(start, size)
        right[rank : 2 * rank, at] = right[0:rank, at]
        whole = size // pass_width

        def column(j, _):
            merge_tile(start + j * pass_width, pass_width)
            return 0

        lax.fori_loop(0, whole, column, 0)
        if size % pass_width:
            merge_tile(start + whole * pass_width, size % pass_width)

    def merge_from(row):
        gather_a(row, row).wait_recv()
        merge_piece((lax.rem(row, 2) * chips + row // 2) * part, part)

    def near(j, _):
        merge_from(lax.rem(chip + j, chips) * 2 + core)
        return 0

    def far(j, _):
        source = lax.rem(chip + j, chips) * 2 + 1 - core
        gather_a(source, source).wait_recv()
        return 0

    own_right.wait()
    merge_piece(slot_of * part, part)
    lax.fori_loop(1, chips, near, 0)
    for k in range(1, rows_count):
        for n in range(3):
            back_copy(n, lax.rem(my_row + k, rows_count), my_row).start()
    lax.fori_loop(0, chips, far, 0)
    merge_piece((1 - core) * half, half)

    for b in range(depth // LANES):
        square = top[b * LANES : (b + 1) * LANES, :]
        top_send[b : b + 1, :] = jnp.max(square.T, axis=0, keepdims=True)

    def gather_top(to, source):
        return remote(
            top_send, got_top.at[source], col_send.at[1, to], col_recv.at[1, source], (my_row, to)
        )

    for k in range(1, cols_count):
        gather_top(lax.rem(my_col + k, cols_count), my_col).start()
    peak = top_send[...]
    for k in range(1, cols_count):
        source = lax.rem(my_col + k, cols_count)
        gather_top(source, source).wait_recv()
        peak = jnp.maximum(peak, got_top[source])
    peak = peak * scale[...] + peak_eps
    fresh[...] = peak / fp8_top
    ratio = scale[...] / peak
    for b in range(depth // LANES):
        inverse[b * LANES : (b + 1) * LANES, :] = jnp.broadcast_to(
            ratio[b : b + 1, :], (LANES, LANES)
        ).T

    for copy in own_back:
        copy.wait()
    core_copy_w.wait_send()
    for c in range(cols_count):
        core_copy_a(c).wait_send()
    for q in range(chips):
        core_copy_b(q).wait_send()
    for k in range(1, chips):
        q = lax.rem(chip + k, chips)
        chip_copy_b(q, chip).wait_send()
        for c in range(cols_count):
            chip_copy_a(q, c, chip).wait_send()
    for k in range(1, cols_count):
        to = lax.rem(my_col + k, cols_count)
        line_copy_a(to, my_col).wait_send()
        line_copy_b(to, my_col).wait_send()
        gather_b(to, my_col).wait_send()
        gather_top(to, my_col).wait_send()
    for k in range(1, rows_count):
        to = lax.rem(my_row + k, rows_count)
        gather_a(to, my_row).wait_send()
        for n in range(3):
            state_copy(n, to, my_row).wait_send()
            back_copy(n, to, to).wait_recv()
            back_copy(n, to, my_row).wait_send()


def finish_kernel(small, merged, inverse, *refs):
    ins, out, outs = refs[:small], refs[small], refs[small + 1 : 2 * small + 1]
    stage, out_sem, small_sem = refs[2 * small + 1 :]
    depth, width = merged.shape
    tile = tile_of(width, decode_width)
    copies = [
        pltpu.make_async_copy(src, dst, small_sem.at[n]) for n, (src, dst) in enumerate(zip(ins, outs))
    ]
    for copy in copies:
        copy.start()

    def put(i):
        slot = lax.rem(i, out_slots)
        return pltpu.make_async_copy(
            stage.at[slot], out.at[pl.ds(pl.multiple_of(i * out_lines, out_lines), out_lines)], out_sem.at[slot]
        )

    steps = depth // out_lines

    def step(i, _):
        slot = lax.rem(i, out_slots)

        @pl.when(i >= out_slots)
        def _():
            put(i - out_slots).wait()

        def column(j, _):
            at = pl.ds(pl.multiple_of(j * tile, LANES), tile)
            for g in range(0, out_lines, 16):
                lines = pl.ds(pl.multiple_of(i * out_lines + g, 16), 16)
                factor = jnp.tile(inverse[lines, :], (1, tile // LANES))
                value = merged[lines, at].astype(jnp.float32) * factor
                stage[slot, g : g + 16, at] = value.astype(jnp.bfloat16)
            return 0

        lax.fori_loop(0, width // tile, column, 0)
        put(i).start()
        return 0

    lax.fori_loop(0, steps, step, 0)

    def drain(i, _):
        put(i).wait()
        return 0

    lax.fori_loop(steps - out_slots, steps, drain, 0)
    for copy in copies:
        copy.wait()


def staged_local(
    fixed_matrix_encodings,
    line_restore_multiplier,
    central_up_matrix,
    central_down_matrix,
    running_mean_up,
    squared_average_up,
    running_mean_down,
    squared_average_down,
    participant_change_up,
    participant_change_down,
    client_tallies,
):
    rows_count = lax.axis_size("row")
    cols_count = lax.axis_size("col")
    count = rows_count * cols_count
    depth, width = fixed_matrix_encodings.shape
    rank_b = central_up_matrix.shape[1]
    rank_a = central_down_matrix.shape[0]
    rank = participant_change_down.shape[1]
    blocks = depth // LANES
    chips = rows_count // 2
    part = width // rows_count
    half = chips * part
    everyone = client_tallies.shape[0] * count
    anywhere = pl.BlockSpec(memory_space=pl.ANY)
    vmem = pl.BlockSpec(memory_space=pltpu.VMEM)
    f32, bf16 = jnp.float32, jnp.bfloat16
    here = pltpu.VMEM
    dma = pltpu.SemaphoreType.DMA
    small_shapes = [(blocks, LANES)] + [(rank_b, depth)] * 3 + [(rank_a, width)] * 3
    outs = pl.pallas_call(
        functools.partial(staged_kernel, rows_count, cols_count, everyone),
        out_shape=[here((depth, width), bf16), here((depth, LANES), f32)]
        + [here(shape, f32) for shape in small_shapes],
        in_specs=[pl.BlockSpec(memory_space=pltpu.SMEM), anywhere] + [vmem] * 4 + [anywhere] * 5,
        out_specs=[vmem] * 9,
        scratch_shapes=[
            here((depth, width), jnp.float8_e4m3fn),
            here((fetch_slots, fetch_lines, width), jnp.int32),
            here((16, LANES), f32),
            here((16, LANES), f32),
            here((cols_count, rank, half), bf16),
            here((cols_count, rank, half), bf16),
            here((chips, cols_count, rank, part), bf16),
            here((chips, cols_count, rank, part), bf16),
            here((cols_count, rank, part), bf16),
            here((cols_count, rank, part), bf16),
            here((rank, part), f32),
            here((chips, rank, depth), bf16),
            here((chips, rank, depth), bf16),
            here((chips, rank, depth), bf16),
            here((chips, rank, depth), bf16),
            here((cols_count, rank_b, depth), f32),
            here((cols_count, rank_b, depth), f32),
            here((3, rows_count, rank_a, part), f32),
            here((3, rows_count, rank_a, part), f32),
            here((rank, part), f32),
            here((rank, part), bf16),
            here((2 * rank, width), bf16),
            here((rank_b, depth), bf16),
            here((cols_count, rank_b, depth), bf16),
            here((2 * rank, depth), f32),
            here((depth, 2 * rank), bf16),
            here((depth, LANES), f32),
            here((blocks, LANES), f32),
            here((cols_count, blocks, LANES), f32),
            dma((fetch_slots,)),
            dma((cols_count + chips + 5,)),
            dma((cols_count + chips + 1,)),
            dma((cols_count + chips + 1,)),
            dma((chips, cols_count + 1)),
            dma((chips, cols_count + 1)),
            dma((2, cols_count)),
            dma((2, cols_count)),
            dma((3, rows_count)),
            dma((3, rows_count)),
            dma((3, rows_count)),
            dma((3, rows_count)),
            dma((rows_count,)),
            dma((rows_count,)),
            dma((2, cols_count)),
            dma((2, cols_count)),
        ],
        compiler_params=pltpu.CompilerParams(
            collective_id=0, has_side_effects=True, vmem_limit_bytes=38_000_000
        ),
    )(
        client_tallies,
        fixed_matrix_encodings,
        line_restore_multiplier.reshape(blocks, LANES),
        central_up_matrix.T,
        running_mean_up.T,
        squared_average_up.T,
        central_down_matrix,
        running_mean_down,
        squared_average_down,
        participant_change_up[0].T,
        participant_change_down[0],
    )
    small = len(small_shapes)
    outs = [pltpu.with_memory_space_constraint(out, pltpu.VMEM) for out in outs]
    normalized, fresh, nb, nmb, nvb, na, nma, nva = pl.pallas_call(
        functools.partial(finish_kernel, small),
        out_shape=[jax.ShapeDtypeStruct((depth, width), bf16)]
        + [jax.ShapeDtypeStruct(shape, f32) for shape in small_shapes],
        in_specs=[vmem] * (2 + small),
        out_specs=[anywhere] * (1 + small),
        scratch_shapes=[
            here((out_slots, out_lines, width), bf16),
            dma((out_slots,)),
            dma((small,)),
        ],
        compiler_params=pltpu.CompilerParams(vmem_limit_bytes=38_000_000),
    )(*outs)
    return (normalized, fresh.reshape(depth), nb.T, na, nmb.T, nvb.T, nma, nva)


def local(*args):
    rows_count, width = lax.axis_size("row"), args[0].shape[1]
    if rows_count % 2 == 0 and width % (rows_count * LANES) == 0:
        return staged_local(*args)
    return direct_local(*args)


def solution(mesh):
    grid = P("row", "col")
    clients = P(("row", "col"), None, None)
    return jax.shard_map(
        local,
        mesh=mesh,
        in_specs=(grid, P("row"), grid, grid, grid, grid, grid, grid, clients, clients, P(("row", "col"), None)),
        out_specs=(grid, P("row"), grid, grid, grid, grid, grid, grid),
        check_vma=False,
    )
```

```python
import functools

import jax
import jax.numpy as jnp
from jax import lax
from jax.experimental import pallas as pl
from jax.experimental.pallas import tpu as pltpu
from jax.sharding import PartitionSpec as P

first_decay = 0.9
second_decay = 0.99
server_rate = 0.1
adam_floor = 0.001
adapter_scale = 2.0
count_scale = 64.0
fp8_top = 448.0
peak_eps = 1e-06
MESH = pl.DeviceIdType.MESH
LANES = 128
decode_lines = 32
merge_lines = 128
code_slots = 3
stage_slots = 2
fetch_lines = 64
fetch_slots = 3
decode_group = 32
decode_width = 3328
pass_width = 512
pass_lines = 32
out_lines = 64
out_slots = 3
decode_plan = (2, 0, 0, 0, 8, 4, 4, 4, 4)


def tile_of(width, limit):
    best = LANES
    for tile in range(LANES, limit + 1, LANES):
        if width % tile == 0:
            best = tile
    return best


def adaptive_update(param, moment, second, grad):
    moment_next = first_decay * moment + (1.0 - first_decay) * grad
    second_next = second_decay * second + (1.0 - second_decay) * grad * grad
    param_next = param - server_rate * moment_next / (jnp.sqrt(second_next) + adam_floor)
    return (param_next, moment_next, second_next)


def scaled_decode(codes):
    low = codes & 127
    mantissa = codes & 7
    mantissa = jnp.where(low > 7, mantissa | 8, mantissa)
    magnitude = mantissa << jnp.maximum(low >> 3, 1)
    return jnp.where(codes > 127, -magnitude, magnitude).astype(jnp.float32)


def merge_kernel(
    rows_count, cols_count,
    codes, scale, pb, mb, vb, pa, ma, va, delta_b, delta_a, weight,
    merged, peak_wide, peak_out, nb, nmb, nvb, na, nma, nva,
    dense, code_buf, got_b, got_a, got_w, fac_b, fac_a, all_b, all_a, wide_b, wide_a,
    left, right, stage, scale_wide, top, top_send, got_top,
    code_sem, out_sem, send_sem, recv_sem, gather_send, gather_recv, own_sem,
):
    my_row, my_col = lax.axis_index("row"), lax.axis_index("col")
    count = rows_count * cols_count
    me = my_row * cols_count + my_col
    depth, width = dense.shape
    steps = depth // decode_lines
    tile = tile_of(width, 1024)
    tiles = width // tile
    rank_b, rank_a = pb.shape[0], pa.shape[0]

    def fetch(i):
        slot = lax.rem(i, code_slots)
        return pltpu.make_async_copy(
            codes.at[pl.ds(i * decode_lines, decode_lines)], code_buf.at[slot], code_sem.at[slot]
        )

    for i in range(code_slots):
        fetch(i).start()

    barrier = pltpu.get_barrier_semaphore()

    def greet(k, _):
        to = lax.rem(me + k, count)
        pl.semaphore_signal(
            barrier, inc=1, device_id=(to // cols_count, lax.rem(to, cols_count)), device_id_type=MESH
        )
        return 0

    lax.fori_loop(1, count, greet, 0)
    pl.semaphore_wait(barrier, count - 1)

    def block_a(row, col):
        return delta_a.at[row, :, pl.ds(pl.multiple_of(col * width, LANES), width)]

    def block_b(row, col):
        return delta_b.at[col, :, pl.ds(pl.multiple_of(row * depth, LANES), depth)]

    def exchange(to, source):
        row, col = to // cols_count, lax.rem(to, cols_count)
        parts = (
            (weight, got_w.at[source]),
            (block_b(row, col), got_b.at[source]),
            (block_a(row, col), got_a.at[source]),
        )
        return [
            pltpu.make_async_remote_copy(
                src_ref=src, dst_ref=dst, send_sem=send_sem.at[n, to], recv_sem=recv_sem.at[n, source],
                device_id=(row, col), device_id_type=MESH,
            )
            for n, (src, dst) in enumerate(parts)
        ]

    def send(k, _):
        for copy in exchange(lax.rem(me + k, count), me):
            copy.start()
        return 0

    lax.fori_loop(1, count, send, 0)
    own = [
        pltpu.make_async_copy(weight, got_w.at[me], own_sem.at[0]),
        pltpu.make_async_copy(block_b(my_row, my_col), got_b.at[me], own_sem.at[1]),
        pltpu.make_async_copy(block_a(my_row, my_col), got_a.at[me], own_sem.at[2]),
    ]
    for copy in own:
        copy.start()

    for b in range(depth // LANES):
        line = jnp.broadcast_to(scale[b : b + 1, :] * 2.0 ** (-10), (LANES, LANES))
        scale_wide[b * LANES : (b + 1) * LANES, :] = line.T

    def decode_step(i, _):
        slot = lax.rem(i, code_slots)
        fetch(i).wait()

        def column(j, _):
            at = pl.ds(pl.multiple_of(j * tile, LANES), tile)
            for g in range(decode_lines // 16):
                value = scaled_decode(code_buf[slot, g * 16 : (g + 1) * 16, at])
                dense[pl.ds(pl.multiple_of(i * decode_lines + g * 16, 16), 16), at] = value.astype(
                    jnp.bfloat16
                )
            return 0

        lax.fori_loop(0, tiles, column, 0)

        @pl.when(i + code_slots < steps)
        def _():
            fetch(i + code_slots).start()

        return 0

    lax.fori_loop(0, steps, decode_step, 0)

    for copy in own:
        copy.wait()

    def arrive(k, _):
        source = lax.rem(me + k, count)
        for copy in exchange(source, source):
            copy.wait_recv()
        return 0

    lax.fori_loop(1, count, arrive, 0)

    def summed(got, which, at, shape):
        def add(s, total):
            return total + got_w[s, which : which + 1, 0:1] * got[s, :, at].astype(jnp.float32)

        return lax.fori_loop(0, count, add, jnp.zeros(shape, jnp.float32), unroll=8)

    grad_b = summed(got_b, 0, slice(None), (rank_b, depth))
    p, m, v = adaptive_update(pb[...], mb[...], vb[...], grad_b)
    nb[...] = p
    nmb[...] = m
    nvb[...] = v
    fac_b[...] = p.astype(jnp.bfloat16)

    def gather_b(to, source):
        return pltpu.make_async_remote_copy(
            src_ref=fac_b, dst_ref=all_b.at[source], send_sem=gather_send.at[0, to],
            recv_sem=gather_recv.at[0, source], device_id=(my_row, to), device_id_type=MESH,
        )

    def gather_a(to, source):
        return pltpu.make_async_remote_copy(
            src_ref=fac_a, dst_ref=all_a.at[source], send_sem=gather_send.at[1, to],
            recv_sem=gather_recv.at[1, source], device_id=(to, my_col), device_id_type=MESH,
        )

    for k in range(1, cols_count):
        gather_b(lax.rem(my_col + k, cols_count), my_col).start()
    own_b = pltpu.make_async_copy(fac_b, all_b.at[my_col], own_sem.at[0])
    own_b.start()

    def update_a(j, _):
        at = pl.ds(pl.multiple_of(j * tile, LANES), tile)
        grad = summed(got_a, 1, at, (rank_a, tile))
        p, m, v = adaptive_update(pa[:, at], ma[:, at], va[:, at], grad)
        na[:, at] = p
        nma[:, at] = m
        nva[:, at] = v
        fac_a[:, at] = p.astype(jnp.bfloat16)
        return 0

    lax.fori_loop(0, tiles, update_a, 0)
    for k in range(1, rows_count):
        gather_a(lax.rem(my_row + k, rows_count), my_row).start()
    own_a = pltpu.make_async_copy(fac_a, all_a.at[my_row], own_sem.at[1])
    own_a.start()

    own_b.wait()
    for k in range(1, cols_count):
        source = lax.rem(my_col + k, cols_count)
        gather_b(source, source).wait_recv()
    for c in range(cols_count):
        wide_b[c * rank_b : (c + 1) * rank_b, :] = all_b[c].astype(jnp.float32)
    left[...] = wide_b[...].T.astype(jnp.bfloat16)

    own_a.wait()
    for k in range(1, rows_count):
        source = lax.rem(my_row + k, rows_count)
        gather_a(source, source).wait_recv()

    def assemble(j, _):
        at = pl.ds(pl.multiple_of(j * tile, LANES), tile)
        for r in range(rows_count):
            wide_a[r * rank_a : (r + 1) * rank_a, :] = all_a[r, :, at].astype(jnp.float32)
        right[:, at] = wide_a[...].astype(jnp.bfloat16)
        return 0

    lax.fori_loop(0, tiles, assemble, 0)

    def put(i):
        slot = lax.rem(i, stage_slots)
        lines = pl.ds(pl.multiple_of(i * merge_lines, merge_lines), merge_lines)
        return pltpu.make_async_copy(stage.at[slot], merged.at[lines], out_sem.at[slot])

    merge_steps = depth // merge_lines

    def merge_step(i, _):
        slot = lax.rem(i, stage_slots)
        lines = pl.ds(pl.multiple_of(i * merge_lines, merge_lines), merge_lines)

        @pl.when(i >= stage_slots)
        def _():
            put(i - stage_slots).wait()

        factor = left[lines, :]
        line_scale = scale_wide[lines, :]

        def column(j, highest):
            for t in range(tile // LANES):
                lane = pl.ds(pl.multiple_of(j * tile + t * LANES, LANES), LANES)
                product = jnp.dot(factor, right[:, lane], preferred_element_type=jnp.float32)
                value = dense[lines, lane].astype(jnp.float32) * line_scale
                value = value + adapter_scale * product
                highest = jnp.maximum(highest, jnp.abs(value))
                stage[slot, :, lane] = value.astype(jnp.bfloat16)
            return highest

        top[lines, :] = lax.fori_loop(
            0, tiles, column, jnp.zeros((merge_lines, LANES), jnp.float32)
        )
        put(i).start()
        return 0

    lax.fori_loop(0, merge_steps, merge_step, 0)

    for b in range(depth // LANES):
        square = top[b * LANES : (b + 1) * LANES, :]
        top_send[b : b + 1, :] = jnp.max(square.T, axis=0, keepdims=True)

    def gather_top(to, source):
        return pltpu.make_async_remote_copy(
            src_ref=top_send, dst_ref=got_top.at[source], send_sem=gather_send.at[2, to],
            recv_sem=gather_recv.at[2, source], device_id=(my_row, to), device_id_type=MESH,
        )

    for k in range(1, cols_count):
        gather_top(lax.rem(my_col + k, cols_count), my_col).start()
    peak = top_send[...]
    for k in range(1, cols_count):
        source = lax.rem(my_col + k, cols_count)
        gather_top(source, source).wait_recv()
        peak = jnp.maximum(peak, got_top[source])
    peak = peak + peak_eps
    peak_out[...] = peak / fp8_top
    for b in range(depth // LANES):
        peak_wide[b * LANES : (b + 1) * LANES, :] = jnp.broadcast_to(
            1.0 / peak[b : b + 1, :], (LANES, LANES)
        ).T

    def drain(i, _):
        put(i).wait()
        return 0

    lax.fori_loop(merge_steps - stage_slots, merge_steps, drain, 0)

    def sent(k, _):
        for copy in exchange(lax.rem(me + k, count), me):
            copy.wait_send()
        return 0

    lax.fori_loop(1, count, sent, 0)
    for k in range(1, cols_count):
        to = lax.rem(my_col + k, cols_count)
        gather_b(to, my_col).wait_send()
        gather_top(to, my_col).wait_send()
    for k in range(1, rows_count):
        gather_a(lax.rem(my_row + k, rows_count), my_row).wait_send()


def normalize_kernel(merged, inverse, out):
    for t in range(merged.shape[1] // LANES):
        at = slice(t * LANES, (t + 1) * LANES)
        out[:, at] = (merged[:, at].astype(jnp.float32) * inverse[...]).astype(jnp.bfloat16)


def direct_local(
    fixed_matrix_encodings,
    line_restore_multiplier,
    central_up_matrix,
    central_down_matrix,
    running_mean_up,
    squared_average_up,
    running_mean_down,
    squared_average_down,
    participant_change_up,
    participant_change_down,
    client_tallies,
):
    rows_count = lax.axis_size("row")
    cols_count = lax.axis_size("col")
    count = rows_count * cols_count
    depth, width = fixed_matrix_encodings.shape
    rank_b = central_up_matrix.shape[1]
    rank_a = central_down_matrix.shape[0]
    rank = participant_change_down.shape[1]
    blocks = depth // LANES
    everyone = client_tallies.shape[0] * count
    weights = client_tallies.astype(jnp.float32) / (count_scale * everyone)
    weight = jnp.broadcast_to(weights[0][:, None], (2, LANES))
    delta_b = participant_change_up[0].T.reshape(cols_count, rank_b, depth * rows_count)
    delta_a = participant_change_down[0].reshape(rows_count, rank_a, width * cols_count)
    anywhere = pl.BlockSpec(memory_space=pl.ANY)
    vmem = pl.BlockSpec(memory_space=pltpu.VMEM)
    f32, bf16 = jnp.float32, jnp.bfloat16
    shape = jax.ShapeDtypeStruct
    outs = pl.pallas_call(
        functools.partial(merge_kernel, rows_count, cols_count),
        out_shape=[
            shape((depth, width), bf16),
            shape((depth, LANES), f32),
            shape((blocks, LANES), f32),
        ]
        + [shape((rank_b, depth), f32)] * 3
        + [shape((rank_a, width), f32)] * 3,
        in_specs=[anywhere] + [vmem] * 7 + [anywhere] * 2 + [vmem],
        out_specs=[anywhere] + [vmem] * 8,
        scratch_shapes=[
            pltpu.VMEM((depth, width), bf16),
            pltpu.VMEM((code_slots, decode_lines, width), jnp.int32),
            pltpu.VMEM((count, rank_b, depth), bf16),
            pltpu.VMEM((count, rank_a, width), bf16),
            pltpu.VMEM((count, 2, LANES), f32),
            pltpu.VMEM((rank_b, depth), bf16),
            pltpu.VMEM((rank_a, width), bf16),
            pltpu.VMEM((cols_count, rank_b, depth), bf16),
            pltpu.VMEM((rows_count, rank_a, width), bf16),
            pltpu.VMEM((rank, depth), f32),
            pltpu.VMEM((rank, tile_of(width, 1024)), f32),
            pltpu.VMEM((depth, rank), bf16),
            pltpu.VMEM((rank, width), bf16),
            pltpu.VMEM((stage_slots, merge_lines, width), bf16),
            pltpu.VMEM((depth, LANES), f32),
            pltpu.VMEM((depth, LANES), f32),
            pltpu.VMEM((blocks, LANES), f32),
            pltpu.VMEM((cols_count, blocks, LANES), f32),
            pltpu.SemaphoreType.DMA((code_slots,)),
            pltpu.SemaphoreType.DMA((stage_slots,)),
            pltpu.SemaphoreType.DMA((3, count)),
            pltpu.SemaphoreType.DMA((3, count)),
            pltpu.SemaphoreType.DMA((3, max(rows_count, cols_count))),
            pltpu.SemaphoreType.DMA((3, max(rows_count, cols_count))),
            pltpu.SemaphoreType.DMA((3,)),
        ],
        compiler_params=pltpu.CompilerParams(
            collective_id=0, has_side_effects=True, vmem_limit_bytes=62_000_000
        ),
    )(
        fixed_matrix_encodings,
        line_restore_multiplier.reshape(blocks, LANES),
        central_up_matrix.T,
        running_mean_up.T,
        squared_average_up.T,
        central_down_matrix,
        running_mean_down,
        squared_average_down,
        delta_b,
        delta_a,
        weight,
    )
    merged, inverse, fresh, nb, nmb, nvb, na, nma, nva = outs
    step = 64
    normalized = pl.pallas_call(
        normalize_kernel,
        grid=(depth // step,),
        out_shape=shape((depth, width), bf16),
        in_specs=[
            pl.BlockSpec((step, width), lambda i: (i, 0)),
            pl.BlockSpec((step, LANES), lambda i: (i, 0)),
        ],
        out_specs=pl.BlockSpec((step, width), lambda i: (i, 0)),
    )(merged, inverse)
    return (normalized, fresh.reshape(depth), nb.T, na, nmb.T, nvb.T, nma, nva)


def packed_decode(codes):
    half = jnp.bfloat16
    value = codes.astype(jnp.float32).astype(half) * half(0.125)
    negative = value > half(15.9)
    value = jnp.where(negative, value - half(16), value)
    power = jnp.floor(jnp.maximum(value, half(1)))
    value = (value - power) + half(1)
    value = jnp.where(negative, -value, value)
    return (value * jnp.exp2(power - half(7))).astype(jnp.float8_e4m3fn)


def staged_kernel(
    rows_count, cols_count, everyone,
    tallies, codes, scale, pb, mb, vb, pa, ma, va, delta_b, delta_a,
    merged, inverse, fresh, nb, nmb, nvb, na, nma, nva,
    dense, code_buf, weight, got_w, mine_a, core_a, pair_a, chip_a, line_a, got_a, sum_a,
    mine_b, core_b, pair_b, chip_b, line_b, got_b,
    state_a, back_a, wide_a, fac_a, right, fac_b, all_b, wide_b, left, top, top_send, got_top,
    code_sem, own_sem, core_send, core_recv, chip_send, chip_recv, line_send, line_recv,
    state_send, state_recv, back_send, back_recv, row_send, row_recv, col_send, col_recv,
):
    my_row, my_col = lax.axis_index("row"), lax.axis_index("col")
    chips = rows_count // 2
    core, chip = lax.rem(my_row, 2), my_row // 2
    depth, width = dense.shape
    rank = delta_a.shape[0]
    rank_b, rank_a = pb.shape[0], pa.shape[0]
    part = width // rows_count
    half = chips * part
    slot_of = core * chips + chip
    tile = tile_of(width, decode_width)
    f32, bf16 = jnp.float32, jnp.bfloat16
    partner = (chip * 2 + 1 - core, my_col)

    def remote(src, dst, send, recv, to):
        return pltpu.make_async_remote_copy(
            src_ref=src, dst_ref=dst, send_sem=send, recv_sem=recv, device_id=to, device_id_type=MESH
        )

    def lanes(start, size):
        return pl.ds(pl.multiple_of(start, LANES), size)

    def fetch(i):
        slot = lax.rem(i, fetch_slots)
        return pltpu.make_async_copy(
            codes.at[pl.ds(i * fetch_lines, fetch_lines)], code_buf.at[slot], code_sem.at[slot]
        )

    steps = depth // fetch_lines
    for i in range(fetch_slots):
        fetch(i).start()

    def own_copies():
        copies = []
        for c in range(cols_count):
            copies.append((delta_a.at[:, lanes(c * width + core * half, half)], mine_a.at[c]))
        for q in range(chips):
            copies.append((delta_b.at[:, lanes((2 * q + core) * depth, depth)], mine_b.at[q]))
        for n, state in enumerate((pa, ma, va)):
            copies.append((state.at[:, lanes(slot_of * part, part)], state_a.at[n, my_row]))
        return [pltpu.make_async_copy(s, d, own_sem.at[n]) for n, (s, d) in enumerate(copies)]

    own = own_copies()
    for copy in own:
        copy.start()

    for n in range(2):
        portion = tallies[0, n].astype(f32) / (count_scale * everyone)
        weight[n * 8 : (n + 1) * 8, :] = jnp.full((8, LANES), portion, f32)

    barrier = pltpu.get_barrier_semaphore()
    for k in range(1, rows_count):
        pl.semaphore_signal(
            barrier, inc=1, device_id=(lax.rem(my_row + k, rows_count), my_col), device_id_type=MESH
        )
    for k in range(1, cols_count):
        pl.semaphore_signal(
            barrier, inc=1, device_id=(my_row, lax.rem(my_col + k, cols_count)), device_id_type=MESH
        )
    pl.semaphore_wait(barrier, rows_count + cols_count - 2)

    def core_copy_a(c):
        return remote(
            delta_a.at[:, lanes(c * width + (1 - core) * half, half)], core_a.at[c],
            core_send.at[c], core_recv.at[c], partner,
        )

    def core_copy_b(q):
        return remote(
            delta_b.at[:, lanes((2 * q + 1 - core) * depth, depth)], core_b.at[q],
            core_send.at[cols_count + q], core_recv.at[cols_count + q], partner,
        )

    last = cols_count + chips
    core_copy_w = remote(weight, got_w, core_send.at[last], core_recv.at[last], partner)

    def state_copy(n, to, source):
        piece = lax.rem(to, 2) * chips + to // 2
        return remote(
            (pa, ma, va)[n].at[:, lanes(piece * part, part)], state_a.at[n, source],
            state_send.at[n, to], state_recv.at[n, source], (to, my_col),
        )

    core_copy_w.start()
    for k in range(1, cols_count + 1):
        core_copy_a(lax.rem(my_col + k, cols_count)).start()
        if k == 1:
            for q in range(chips):
                core_copy_b(q).start()
    for k in range(1, rows_count):
        for n in range(3):
            state_copy(n, lax.rem(my_row + k, rows_count), my_row).start()

    splits = 2 if width // tile % 2 == 0 else 1
    share = width // tile // splits

    def decode_step(unit, _):
        i, turn = unit // splits, lax.rem(unit, splits)
        slot = lax.rem(i, fetch_slots)

        @pl.when(turn == 0)
        def _():
            fetch(i).wait()

        def column(j, _):
            at = lanes((turn * share + j) * tile, tile)
            for g in range(fetch_lines // decode_group):
                start = pl.multiple_of(i * fetch_lines + g * decode_group, decode_group)
                dense[pl.ds(start, decode_group), at] = packed_decode(
                    code_buf[slot, g * decode_group : (g + 1) * decode_group, at]
                )
            return 0

        lax.fori_loop(0, share, column, 0)

        @pl.when((i + fetch_slots < steps) & (turn == splits - 1))
        def _():
            fetch(i + fetch_slots).start()

        return 0

    done = [0]
    plan = list(decode_plan)
    units = steps * splits

    def decode_some():
        until = min(units, done[0] + plan.pop(0)) if plan else units
        if until > done[0]:
            lax.fori_loop(done[0], until, decode_step, 0)
        done[0] = until

    decode_some()

    for copy in own:
        copy.wait()
    core_copy_w.wait_recv()

    def blend(mine, theirs, which):
        ours = weight[which * 8 : which * 8 + 1, 0:1] * mine.astype(f32)
        return (ours + got_w[which * 8 : which * 8 + 1, 0:1] * theirs.astype(f32)).astype(bf16)

    def chip_copy_a(q, c, source):
        return remote(
            pair_a.at[q, c], chip_a.at[source, c], chip_send.at[q, c], chip_recv.at[source, c],
            (q * 2 + core, my_col),
        )

    def chip_copy_b(q, source):
        return remote(
            pair_b.at[q], chip_b.at[source], chip_send.at[q, cols_count],
            chip_recv.at[source, cols_count], (q * 2 + core, my_col),
        )

    for k in range(1, cols_count + 1):
        c = lax.rem(my_col + k, cols_count)
        core_copy_a(c).wait_recv()
        for q in range(chips):
            at = slice(q * part, (q + 1) * part)
            pair_a[q, c] = blend(mine_a[c, :, at], core_a[c, :, at], 1)
        for j in range(1, chips):
            chip_copy_a(lax.rem(chip + j, chips), c, chip).start()
        if k == 1:
            for q in range(chips):
                core_copy_b(q).wait_recv()
                pair_b[q] = blend(mine_b[q], core_b[q], 0)
            for j in range(1, chips):
                chip_copy_b(lax.rem(chip + j, chips), chip).start()
        decode_some()

    def line_copy_a(c, source):
        return remote(
            line_a.at[c], got_a.at[source], line_send.at[0, c], line_recv.at[0, source], (my_row, c)
        )

    def line_copy_b(c, source):
        return remote(
            line_b.at[c], got_b.at[source], line_send.at[1, c], line_recv.at[1, source], (my_row, c)
        )

    def sum_b():
        total = pair_b[chip].astype(f32)
        for k in range(1, chips):
            source = lax.rem(chip + k, chips)
            chip_copy_b(source, source).wait_recv()
            total = total + chip_b[source].astype(f32)
        for c in range(cols_count):
            line_b[c] = total[c * rank_b : (c + 1) * rank_b, :]
        for k in range(1, cols_count):
            line_copy_b(lax.rem(my_col + k, cols_count), my_col).start()

    for k in range(1, cols_count + 1):
        c = lax.rem(my_col + k, cols_count)
        total = pair_a[chip, c].astype(f32)
        for j in range(1, chips):
            source = lax.rem(chip + j, chips)
            chip_copy_a(source, c, source).wait_recv()
            total = total + chip_a[source, c].astype(f32)
        if k < cols_count:
            line_a[c] = total.astype(bf16)
            line_copy_a(c, my_col).start()
            if k == 1:
                sum_b()
            decode_some()
        else:
            sum_a[...] = total

    decode_some()

    grad = line_b[my_col]
    for k in range(1, cols_count):
        source = lax.rem(my_col + k, cols_count)
        line_copy_b(source, source).wait_recv()
        grad = grad + got_b[source]
    p, m, v = adaptive_update(pb[...], mb[...], vb[...], grad)
    nb[...] = p
    nmb[...] = m
    nvb[...] = v
    fac_b[...] = p.astype(bf16)

    def gather_b(to, source):
        return remote(
            fac_b, all_b.at[source], col_send.at[0, to], col_recv.at[0, source], (my_row, to)
        )

    for k in range(1, cols_count):
        gather_b(lax.rem(my_col + k, cols_count), my_col).start()

    for k in range(1, rows_count):
        for n in range(3):
            source = lax.rem(my_row + k, rows_count)
            state_copy(n, source, source).wait_recv()
    for k in range(1, cols_count):
        source = lax.rem(my_col + k, cols_count)
        line_copy_a(source, source).wait_recv()

    grad = sum_a[...]
    for k in range(1, cols_count):
        grad = grad + got_a[lax.rem(my_col + k, cols_count)].astype(f32)
    for r in range(rows_count):
        at = slice(r * rank_a, (r + 1) * rank_a)
        p, m, v = adaptive_update(state_a[0, r], state_a[1, r], state_a[2, r], grad[at, :])
        back_a[0, r] = p
        back_a[1, r] = m
        back_a[2, r] = v
        wide_a[at, :] = p
    fac_a[...] = wide_a[...].astype(bf16)

    def right_at(row):
        piece = lax.rem(row, 2) * chips + row // 2
        return right.at[0:rank, lanes(piece * part, part)]

    def gather_a(to, source):
        return remote(
            fac_a, right_at(source), row_send.at[to], row_recv.at[source], (to, my_col)
        )

    def back_copy(n, to, source):
        piece = lax.rem(source, 2) * chips + source // 2
        return remote(
            back_a.at[n, to], (na, nma, nva)[n].at[:, lanes(piece * part, part)],
            back_send.at[n, to], back_recv.at[n, source], (to, my_col),
        )

    for j in range(1, chips):
        gather_a(lax.rem(chip + j, chips) * 2 + core, my_row).start()
    for j in range(chips):
        gather_a(lax.rem(chip + j, chips) * 2 + 1 - core, my_row).start()
    own_right = pltpu.make_async_copy(fac_a, right_at(my_row), own_sem.at[0])
    own_right.start()
    own_factor = pltpu.make_async_copy(fac_b, all_b.at[my_col], own_sem.at[1])
    own_factor.start()
    own_back = [
        pltpu.make_async_copy(
            back_a.at[n, my_row], ref.at[:, lanes(slot_of * part, part)], own_sem.at[2 + n]
        )
        for n, ref in enumerate((na, nma, nva))
    ]
    for copy in own_back:
        copy.start()

    plan[:] = []
    decode_some()

    own_factor.wait()
    for k in range(1, cols_count):
        source = lax.rem(my_col + k, cols_count)
        gather_b(source, source).wait_recv()
    for c in range(cols_count):
        wide_b[c * rank_b : (c + 1) * rank_b, :] = all_b[c].astype(f32)
    for b in range(depth // LANES):
        at = slice(b * LANES, (b + 1) * LANES)
        folded = wide_b[0:rank, at] * (adapter_scale / scale[b : b + 1, :])
        high = folded.astype(bf16).astype(f32)
        wide_b[0:rank, at] = high
        wide_b[rank : 2 * rank, at] = folded - high
    left[...] = wide_b[...].T.astype(bf16)

    top[...] = jnp.zeros((depth, LANES), f32)

    def merge_tile(at, size):
        for lines in range(0, depth, 1024):
            deep = min(1024, depth - lines)
            product = jnp.dot(
                left[lines : lines + deep, :], right[:, lanes(at, size)], preferred_element_type=f32
            )
            for g in range(0, deep, pass_lines):
                here = slice(lines + g, lines + g + pass_lines)
                highest = top[here, :]
                for t in range(0, size, LANES):
                    lane = lanes(at + t, LANES)
                    value = product[g : g + pass_lines, t : t + LANES] + dense[here, lane].astype(f32)
                    highest = jnp.maximum(highest, jnp.abs(value))
                    merged[here, lane] = value.astype(bf16)
                top[here, :] = highest

    def merge_piece(start, size):
        at = lanes(start, size)
        right[rank : 2 * rank, at] = right[0:rank, at]
        whole = size // pass_width

        def column(j, _):
            merge_tile(start + j * pass_width, pass_width)
            return 0

        lax.fori_loop(0, whole, column, 0)
        if size % pass_width:
            merge_tile(start + whole * pass_width, size % pass_width)

    def merge_from(row):
        gather_a(row, row).wait_recv()
        merge_piece((lax.rem(row, 2) * chips + row // 2) * part, part)

    def near(j, _):
        merge_from(lax.rem(chip + j, chips) * 2 + core)
        return 0

    def far(j, _):
        source = lax.rem(chip + j, chips) * 2 + 1 - core
        gather_a(source, source).wait_recv()
        return 0

    own_right.wait()
    merge_piece(slot_of * part, part)
    lax.fori_loop(1, chips, near, 0)
    for k in range(1, rows_count):
        for n in range(3):
            back_copy(n, lax.rem(my_row + k, rows_count), my_row).start()
    lax.fori_loop(0, chips, far, 0)
    merge_piece((1 - core) * half, half)

    for b in range(depth // LANES):
        square = top[b * LANES : (b + 1) * LANES, :]
        top_send[b : b + 1, :] = jnp.max(square.T, axis=0, keepdims=True)

    def gather_top(to, source):
        return remote(
            top_send, got_top.at[source], col_send.at[1, to], col_recv.at[1, source], (my_row, to)
        )

    for k in range(1, cols_count):
        gather_top(lax.rem(my_col + k, cols_count), my_col).start()
    peak = top_send[...]
    for k in range(1, cols_count):
        source = lax.rem(my_col + k, cols_count)
        gather_top(source, source).wait_recv()
        peak = jnp.maximum(peak, got_top[source])
    peak = peak * scale[...] + peak_eps
    fresh[...] = peak / fp8_top
    ratio = scale[...] / peak
    for b in range(depth // LANES):
        inverse[b * LANES : (b + 1) * LANES, :] = jnp.broadcast_to(
            ratio[b : b + 1, :], (LANES, LANES)
        ).T

    for copy in own_back:
        copy.wait()
    core_copy_w.wait_send()
    for c in range(cols_count):
        core_copy_a(c).wait_send()
    for q in range(chips):
        core_copy_b(q).wait_send()
    for k in range(1, chips):
        q = lax.rem(chip + k, chips)
        chip_copy_b(q, chip).wait_send()
        for c in range(cols_count):
            chip_copy_a(q, c, chip).wait_send()
    for k in range(1, cols_count):
        to = lax.rem(my_col + k, cols_count)
        line_copy_a(to, my_col).wait_send()
        line_copy_b(to, my_col).wait_send()
        gather_b(to, my_col).wait_send()
        gather_top(to, my_col).wait_send()
    for k in range(1, rows_count):
        to = lax.rem(my_row + k, rows_count)
        gather_a(to, my_row).wait_send()
        for n in range(3):
            state_copy(n, to, my_row).wait_send()
            back_copy(n, to, to).wait_recv()
            back_copy(n, to, my_row).wait_send()


def finish_kernel(small, merged, inverse, *refs):
    ins, out, outs = refs[:small], refs[small], refs[small + 1 : 2 * small + 1]
    stage, out_sem, small_sem = refs[2 * small + 1 :]
    depth, width = merged.shape
    tile = tile_of(width, decode_width)
    copies = [
        pltpu.make_async_copy(src, dst, small_sem.at[n]) for n, (src, dst) in enumerate(zip(ins, outs))
    ]
    for copy in copies:
        copy.start()

    def put(i):
        slot = lax.rem(i, out_slots)
        return pltpu.make_async_copy(
            stage.at[slot], out.at[pl.ds(pl.multiple_of(i * out_lines, out_lines), out_lines)], out_sem.at[slot]
        )

    steps = depth // out_lines

    def step(i, _):
        slot = lax.rem(i, out_slots)

        @pl.when(i >= out_slots)
        def _():
            put(i - out_slots).wait()

        def column(j, _):
            at = pl.ds(pl.multiple_of(j * tile, LANES), tile)
            for g in range(0, out_lines, 16):
                lines = pl.ds(pl.multiple_of(i * out_lines + g, 16), 16)
                factor = jnp.tile(inverse[lines, :], (1, tile // LANES))
                value = merged[lines, at].astype(jnp.float32) * factor
                stage[slot, g : g + 16, at] = value.astype(jnp.bfloat16)
            return 0

        lax.fori_loop(0, width // tile, column, 0)
        put(i).start()
        return 0

    lax.fori_loop(0, steps, step, 0)

    def drain(i, _):
        put(i).wait()
        return 0

    lax.fori_loop(steps - out_slots, steps, drain, 0)
    for copy in copies:
        copy.wait()


def staged_local(
    fixed_matrix_encodings,
    line_restore_multiplier,
    central_up_matrix,
    central_down_matrix,
    running_mean_up,
    squared_average_up,
    running_mean_down,
    squared_average_down,
    participant_change_up,
    participant_change_down,
    client_tallies,
):
    rows_count = lax.axis_size("row")
    cols_count = lax.axis_size("col")
    count = rows_count * cols_count
    depth, width = fixed_matrix_encodings.shape
    rank_b = central_up_matrix.shape[1]
    rank_a = central_down_matrix.shape[0]
    rank = participant_change_down.shape[1]
    blocks = depth // LANES
    chips = rows_count // 2
    part = width // rows_count
    half = chips * part
    everyone = client_tallies.shape[0] * count
    anywhere = pl.BlockSpec(memory_space=pl.ANY)
    vmem = pl.BlockSpec(memory_space=pltpu.VMEM)
    f32, bf16 = jnp.float32, jnp.bfloat16
    here = pltpu.VMEM
    dma = pltpu.SemaphoreType.DMA
    small_shapes = [(blocks, LANES)] + [(rank_b, depth)] * 3 + [(rank_a, width)] * 3
    outs = pl.pallas_call(
        functools.partial(staged_kernel, rows_count, cols_count, everyone),
        out_shape=[here((depth, width), bf16), here((depth, LANES), f32)]
        + [here(shape, f32) for shape in small_shapes],
        in_specs=[pl.BlockSpec(memory_space=pltpu.SMEM), anywhere] + [vmem] * 4 + [anywhere] * 5,
        out_specs=[vmem] * 9,
        scratch_shapes=[
            here((depth, width), jnp.float8_e4m3fn),
            here((fetch_slots, fetch_lines, width), jnp.int32),
            here((16, LANES), f32),
            here((16, LANES), f32),
            here((cols_count, rank, half), bf16),
            here((cols_count, rank, half), bf16),
            here((chips, cols_count, rank, part), bf16),
            here((chips, cols_count, rank, part), bf16),
            here((cols_count, rank, part), bf16),
            here((cols_count, rank, part), bf16),
            here((rank, part), f32),
            here((chips, rank, depth), bf16),
            here((chips, rank, depth), bf16),
            here((chips, rank, depth), bf16),
            here((chips, rank, depth), bf16),
            here((cols_count, rank_b, depth), f32),
            here((cols_count, rank_b, depth), f32),
            here((3, rows_count, rank_a, part), f32),
            here((3, rows_count, rank_a, part), f32),
            here((rank, part), f32),
            here((rank, part), bf16),
            here((2 * rank, width), bf16),
            here((rank_b, depth), bf16),
            here((cols_count, rank_b, depth), bf16),
            here((2 * rank, depth), f32),
            here((depth, 2 * rank), bf16),
            here((depth, LANES), f32),
            here((blocks, LANES), f32),
            here((cols_count, blocks, LANES), f32),
            dma((fetch_slots,)),
            dma((cols_count + chips + 5,)),
            dma((cols_count + chips + 1,)),
            dma((cols_count + chips + 1,)),
            dma((chips, cols_count + 1)),
            dma((chips, cols_count + 1)),
            dma((2, cols_count)),
            dma((2, cols_count)),
            dma((3, rows_count)),
            dma((3, rows_count)),
            dma((3, rows_count)),
            dma((3, rows_count)),
            dma((rows_count,)),
            dma((rows_count,)),
            dma((2, cols_count)),
            dma((2, cols_count)),
        ],
        compiler_params=pltpu.CompilerParams(
            collective_id=0, has_side_effects=True, vmem_limit_bytes=38_000_000
        ),
    )(
        client_tallies,
        fixed_matrix_encodings,
        line_restore_multiplier.reshape(blocks, LANES),
        central_up_matrix.T,
        running_mean_up.T,
        squared_average_up.T,
        central_down_matrix,
        running_mean_down,
        squared_average_down,
        participant_change_up[0].T,
        participant_change_down[0],
    )
    small = len(small_shapes)
    outs = [pltpu.with_memory_space_constraint(out, pltpu.VMEM) for out in outs]
    normalized, fresh, nb, nmb, nvb, na, nma, nva = pl.pallas_call(
        functools.partial(finish_kernel, small),
        out_shape=[jax.ShapeDtypeStruct((depth, width), bf16)]
        + [jax.ShapeDtypeStruct(shape, f32) for shape in small_shapes],
        in_specs=[vmem] * (2 + small),
        out_specs=[anywhere] * (1 + small),
        scratch_shapes=[
            here((out_slots, out_lines, width), bf16),
            dma((out_slots,)),
            dma((small,)),
        ],
        compiler_params=pltpu.CompilerParams(vmem_limit_bytes=38_000_000),
    )(*outs)
    return (normalized, fresh.reshape(depth), nb.T, na, nmb.T, nvb.T, nma, nva)


def local(*args):
    rows_count, width = lax.axis_size("row"), args[0].shape[1]
    if rows_count % 2 == 0 and width % (rows_count * LANES) == 0:
        return staged_local(*args)
    return direct_local(*args)


def solution(mesh):
    grid = P("row", "col")
    clients = P(("row", "col"), None, None)
    return jax.shard_map(
        local,
        mesh=mesh,
        in_specs=(grid, P("row"), grid, grid, grid, grid, grid, grid, clients, clients, P(("row", "col"), None)),
        out_specs=(grid, P("row"), grid, grid, grid, grid, grid, grid),
        check_vma=False,
    )
```
